32 devices in a mesh: fault: 16 (over z, y, core), off: 2 (over x).
Axes of the slice: x: 2, y: 2, z: 4, core: 2. Of those that a mesh axis runs over, the one named last changes fastest.
Arguments:
- modal_state: float32 [9, 56, 1024], P(None, None, ('fault', 'off')), may hold values from -6 to 6
- star_mats: float32 [3, 9, 9, 1024], P(None, None, None, ('fault', 'off')), may hold values from -2 to 2
- flux_local: float32 [4, 9, 9, 1024], P(None, None, None, ('fault', 'off')), may hold values from -1 to 1
- flux_nbr: float32 [4, 9, 9, 1024], P(None, None, None, ('fault', 'off')), may hold values from -1 to 1
- stiff_time: float32 [3, 56, 56], replicated, may hold values from -0.75 to 0.75
- stiff_vol: float32 [3, 56, 56], replicated, may hold values from -0.375 to 0.375
- flux_minus: float32 [4, 56, 56], replicated, may hold values from -0.375 to 0.375
- face_proj: float32 [4, 56, 21], replicated, may hold values from -0.75 to 0.75
- face_turn: float32 [3, 21, 21], replicated, may hold values from -1.25 to 1.25
- face_lift: float32 [4, 21, 56], replicated, may hold values from -0.625 to 0.625
- cluster: int32 [1024], P(('fault', 'off')), may hold values from 0 to 1, as said below
- send_elem: int32 [16, 2, 52], P('fault', 'off'), may hold values from 0 to 31
- send_face: int32 [16, 2, 52], P('fault', 'off'), may hold values from 0 to 3
- nbr_index: int32 [4, 1024], P(None, ('fault', 'off')), may hold values from 0 to 179, as said below
- orientation: int32 [4, 1024], P(None, ('fault', 'off')), may hold values from 0 to 2
- source_elem: int32 [16], replicated, may hold values from 0 to 1023
- source_term: float32 [16, 9, 56], replicated, may hold values from -6 to 6
Outputs:
- new_state: float32 [9, 56, 1024], P(None, None, ('fault', 'off'))
The draws below stay inside these ranges and needn't reach their ends.
Inputs may be any that keep to these rules, and one draw needn't show every extreme that they name: `cluster`: each device holds at most 16 fine elements, and some device exactly 16 in every draw. `nbr_index`: on each device, entries below 128 name the device's own face traces; every received entry 128 .. 179 is named by exactly one face of the device.
All inputs are finite; a program needn't handle non-finite values.
Results may differ from the reference program's by a relative error of at most 0.0003.
Values sent between devices are 32-bit elements; how exact they have to be, the bound alone decides.
No kernel may reach another device: no remote copies, remote signals or barrier semaphores. Data moves between devices by JAX's collectives and lax.ppermute only.
A program may use at most 64 MiB of HBM per device.

```python
import math
import jax
import jax.numpy as jnp
from jax import lax

QUANT = 9
MODES = 56
FACE_MODES = 21
TERMS = 6
SOURCES = 16
E_DEV = 32
SF = 16
SO = 10
SLOTS = 52
FINE_MAX = 16
E_TOTAL = 1024
N_FAULT = 16
N_OFF = 2


def draw_cluster(key, part):
    blocks = E_TOTAL // E_DEV
    key_count, key_block, key_perm = jax.random.split(key, 3)
    counts = jax.random.randint(key_count, (blocks,), FINE_MAX // 4, FINE_MAX + 1)
    full_block = jax.random.randint(key_block, (), 0, blocks)
    counts = jnp.where(jnp.arange(blocks) == full_block, FINE_MAX, counts)
    block_keys = jax.random.split(key_perm, blocks)
    ranking = jax.vmap(lambda sub_key: jax.random.permutation(sub_key, E_DEV))(block_keys).astype(jnp.int32)
    marked = (ranking < counts[:, None]).astype(jnp.int32)
    return marked.reshape(E_TOTAL)


def draw_nbr_index(key, part):
    blocks = E_TOTAL // E_DEV
    local_count = 4 * E_DEV
    key_perm, key_pick = jax.random.split(key)
    block_keys = jax.random.split(key_perm, blocks)
    ranking = jax.vmap(lambda sub_key: jax.random.permutation(sub_key, local_count))(block_keys).astype(jnp.int32)
    picks = jax.random.randint(key_pick, (blocks, local_count), 0, local_count)
    chosen = jnp.where(ranking < SLOTS, local_count + ranking, picks).astype(jnp.int32)
    return chosen.reshape(blocks, 4, E_DEV).transpose(1, 0, 2).reshape(4, E_TOTAL)


def touch_ends(values, rng, low, top_value):
    longest = values.shape.index(max(values.shape))
    spots = []
    for shift in (0, 1):
        where = [jax.random.randint(jax.random.fold_in(rng, axis), (), 0, length) for axis, length in enumerate(values.shape)]
        where[longest] = (where[longest] + shift) % values.shape[longest]
        spots.append(tuple(where))
    return values.at[spots[0]].set(low).at[spots[1]].set(top_value)


def levels(key, dims, cuts, smallest, largest):
    def one(dim, blocks):
        steps = jax.random.uniform(jax.random.fold_in(jax.random.fold_in(key, 6), dim), (blocks,), jnp.float32, smallest / len(cuts), largest / len(cuts))
        return jnp.repeat(jnp.exp(steps), dims[dim] // blocks).reshape((-1,) + (1,) * (len(dims) - dim - 1))

    gain = one(*cuts[0])
    for cut in cuts[1:]:
        gain = gain * one(*cut)
    return gain


def scatter_about(key, shape, deviation, most, shards=(), dtype=jnp.bfloat16):
    gain = levels(key, shape, shards, -0.22, 0.18) if shards else 1.0
    values = jax.random.normal(key, shape, jnp.float32) * deviation * gain
    return jnp.minimum(jnp.maximum(values, -most), most).astype(dtype)


def setup_inputs(seed: int = 0) -> dict:
    key_list = jax.random.split(jax.random.key(seed), 18)
    return {
        "modal_state": scatter_about(key_list[0], (QUANT, MODES, E_TOTAL), 1.0, 6.0, ((2, 32),), jnp.float32),
        "star_mats": scatter_about(key_list[1], (3, QUANT, QUANT, E_TOTAL), QUANT ** -0.5, 2.0, ((3, 32),), jnp.float32),
        "flux_local": scatter_about(key_list[2], (4, QUANT, QUANT, E_TOTAL), (4 * QUANT) ** -0.5, 1.0, ((3, 32),), jnp.float32),
        "flux_nbr": scatter_about(key_list[3], (4, QUANT, QUANT, E_TOTAL), (4 * QUANT) ** -0.5, 1.0, ((3, 32),), jnp.float32),
        "stiff_time": scatter_about(key_list[4], (3, MODES, MODES), MODES ** -0.5, 0.75, (), jnp.float32),
        "stiff_vol": scatter_about(key_list[5], (3, MODES, MODES), (4 * MODES) ** -0.5, 0.375, (), jnp.float32),
        "flux_minus": scatter_about(key_list[6], (4, MODES, MODES), (4 * MODES) ** -0.5, 0.375, (), jnp.float32),
        "face_proj": scatter_about(key_list[7], (4, MODES, FACE_MODES), MODES ** -0.5, 0.75, (), jnp.float32),
        "face_turn": scatter_about(key_list[8], (3, FACE_MODES, FACE_MODES), FACE_MODES ** -0.5, 1.25, (), jnp.float32),
        "face_lift": scatter_about(key_list[9], (4, FACE_MODES, MODES), (4 * FACE_MODES) ** -0.5, 0.625, (), jnp.float32),
        "cluster": draw_cluster(jax.random.fold_in(key_list[17], 71), 0),
        "send_elem": touch_ends(jax.random.randint(key_list[11], (N_FAULT, N_OFF, SLOTS), 0, E_DEV), jax.random.fold_in(key_list[11], 1), 0, E_DEV - 1).astype(jnp.int32),
        "send_face": touch_ends(jax.random.randint(key_list[12], (N_FAULT, N_OFF, SLOTS), 0, 4), jax.random.fold_in(key_list[12], 1), 0, 3).astype(jnp.int32),
        "nbr_index": draw_nbr_index(jax.random.fold_in(key_list[17], 71), 0),
        "orientation": touch_ends(jax.random.randint(key_list[14], (4, E_TOTAL), 0, 3), jax.random.fold_in(key_list[14], 1), 0, 2).astype(jnp.int32),
        "source_elem": touch_ends(jax.random.randint(key_list[15], (SOURCES,), 0, E_TOTAL), jax.random.fold_in(key_list[15], 1), 0, E_TOTAL - 1).astype(jnp.int32),
        "source_term": scatter_about(key_list[16], (SOURCES, QUANT, MODES), 1.0, 6.0, (), jnp.float32),
    }


PRECISE = lax.Precision.HIGHEST
HALF_STEP = 0.5


def weights_over(start, finish):
    return [(finish ** (degree + 1) - start ** (degree + 1)) / math.factorial(degree + 1) for degree in range(TERMS)]


def derive(modal_in, star_mats, stiffness):
    stiffened = jnp.einsum('pme,dmn->dpne', modal_in, stiffness, precision=PRECISE)
    return jnp.einsum('dqpe,dpne->qne', star_mats, stiffened, precision=PRECISE)


def predict(modal_in, star_mats, stiff_time):
    series = [modal_in]
    for degree in range(1, TERMS):
        series.append(derive(series[-1], star_mats, stiff_time))
    return series


def integrate(series, weights):
    summed = weights[0] * series[0]
    for degree in range(1, TERMS):
        summed = summed + weights[degree] * series[degree]
    return summed


def traces(integral, face_proj):
    faced = jnp.einsum('qme,fmj->qjfe', integral, face_proj, precision=PRECISE)
    return faced.reshape(faced.shape[0], faced.shape[1], 4 * integral.shape[2])


def update(base_state, integral, neighbours, star_mats, flux_local, flux_nbr, stiff_vol, flux_minus, face_turn, face_lift, orientation):
    volume = derive(integral, star_mats, stiff_vol)
    face_flux = jnp.einsum('pme,fmn->fpne', integral, flux_minus, precision=PRECISE)
    local_part = jnp.einsum('fqpe,fpne->qne', flux_local, face_flux, precision=PRECISE)
    rotated = [jnp.einsum('qife,ij->qjfe', neighbours, face_turn[facing], precision=PRECISE) for facing in range(3)]
    facing_now = orientation[None, None]
    turned = jnp.where(facing_now == 0, rotated[0], jnp.where(facing_now == 1, rotated[1], rotated[2]))
    lifted = jnp.einsum('qjfe,fjn->fqne', turned, face_lift, precision=PRECISE)
    nbr_part = jnp.einsum('fqpe,fpne->qne', flux_nbr, lifted, precision=PRECISE)
    return base_state + volume + local_part + nbr_part


def receive(outgoing):
    blocks = outgoing.shape[0]
    quant, face_modes = outgoing.shape[1], outgoing.shape[2]
    grid = outgoing.reshape(N_FAULT, N_OFF, quant, face_modes, SLOTS)
    rim_slots = grid[..., :2 * SF]
    lower = jnp.roll(rim_slots, 1, axis=0)[..., SF:]
    upper = jnp.roll(rim_slots, -1, axis=0)[..., :SF]
    off_part = grid[..., 2 * SF:].reshape(N_FAULT, N_OFF, quant, face_modes, N_OFF, SO)
    arrived = jnp.transpose(off_part, (0, 4, 2, 3, 1, 5)).reshape(N_FAULT, N_OFF, quant, face_modes, N_OFF * SO)
    ghosts = jnp.concatenate([lower, upper, arrived], axis=-1)
    return ghosts.reshape(blocks, quant, face_modes, SLOTS)


def reference(modal_state, star_mats, flux_local, flux_nbr, stiff_time, stiff_vol, flux_minus, face_proj, face_turn, face_lift, cluster, send_elem, send_face, nbr_index, orientation, source_elem, source_term):
    blocks = E_TOTAL // E_DEV

    def to_blocks(array):
        shaped = array.reshape(array.shape[:-1] + (blocks, E_DEV))
        return jnp.moveaxis(shaped, -2, 0)

    state_b = to_blocks(modal_state)
    star_b = to_blocks(star_mats)
    local_b = to_blocks(flux_local)
    nbr_b = to_blocks(flux_nbr)
    cluster_b = to_blocks(cluster)
    index_b = to_blocks(nbr_index)
    orient_b = to_blocks(orientation)
    elems_b = send_elem.reshape(blocks, SLOTS)
    faces_b = send_face.reshape(blocks, SLOTS)
    early = weights_over(0.0, HALF_STEP)
    late = weights_over(HALF_STEP, 1.0)

    def phase_one(inputs):
        state_in, star_in, elems_in, faces_in = inputs
        series = predict(state_in, star_in, stiff_time)
        first_half = integrate(series, early)
        second_half = integrate(series, late)
        table_in = traces(first_half, face_proj)
        return first_half, second_half, table_in, jnp.take(table_in, faces_in * E_DEV + elems_in, axis=2)

    first_b, second_b, table_one, sent_one = lax.map(phase_one, (state_b, star_b, elems_b, faces_b))
    ghosts_one = receive(sent_one)

    def phase_two(inputs):
        (state_in, star_in, local_in, nbr_in, cluster_in, index_in, orient_in, first_half, second_half, table_in, ghosts_in, elems_in, faces_in) = inputs
        combined = jnp.concatenate([table_in, ghosts_in], axis=2)
        near_first = jnp.take(combined, index_in, axis=2)
        is_fine = (cluster_in == 1)[None, None, :]
        stepped = update(state_in, first_half, near_first, star_in, local_in, nbr_in, stiff_vol, flux_minus, face_turn, face_lift, orient_in)
        half_state = jnp.where(is_fine, stepped, state_in)
        second_fine = integrate(predict(half_state, star_in, stiff_time), early)
        later_part = jnp.where(is_fine, second_fine, second_half)
        table_out = traces(later_part, face_proj)
        return half_state, later_part, near_first, table_out, jnp.take(table_out, faces_in * E_DEV + elems_in, axis=2)

    half_b, later_b, near_b, table_two, sent_two = lax.map(phase_two, (state_b, star_b, local_b, nbr_b, cluster_b, index_b, orient_b, first_b, second_b, table_one, ghosts_one, elems_b, faces_b))
    ghosts_two = receive(sent_two)

    def phase_three(inputs):
        (state_in, star_in, local_in, nbr_in, cluster_in, index_in, orient_in, first_half, second_half, half_state, later_part, near_first, table_in, ghosts_in) = inputs
        combined = jnp.concatenate([table_in, ghosts_in], axis=2)
        near_second = jnp.take(combined, index_in, axis=2)
        is_fine = (cluster_in == 1)[None, None, :]
        neighbours = jnp.where(is_fine, near_second, near_first + near_second)
        base_state = jnp.where(is_fine, half_state, state_in)
        integral = jnp.where(is_fine, later_part, first_half + second_half)
        return update(base_state, integral, neighbours, star_in, local_in, nbr_in, stiff_vol, flux_minus, face_turn, face_lift, orient_in)

    final_b = lax.map(phase_three, (state_b, star_b, local_b, nbr_b, cluster_b, index_b, orient_b, first_b, second_b, half_b, later_b, near_b, table_two, ghosts_two))
    stepped_all = jnp.moveaxis(final_b, 0, -2).reshape(final_b.shape[1], final_b.shape[2], E_TOTAL)
    return stepped_all.at[:, :, source_elem].add(jnp.transpose(source_term, (1, 2, 0)))
```

```python
import functools
import math

import jax
import jax.numpy as jnp
from jax import lax
from jax.experimental import pallas as pl
from jax.experimental.pallas import tpu as pltpu
from jax.sharding import PartitionSpec as P

Q = 9
M = 56
J = 21
JP = 24
E = 32
LANES = 128
W = 384
SF = 16
SO = 10
SRC = 16
TERMS = 6
EARLY = [0.5 ** (k + 1) / math.factorial(k + 1) for k in range(TERMS)]
LATE = [(1.0 - 0.5 ** (k + 1)) / math.factorial(k + 1) for k in range(TERMS)]
F32 = jnp.float32
BF16 = jnp.bfloat16
TAB = 256


def lane_iota(rows, width=LANES):
    return lax.broadcasted_iota(jnp.int32, (rows, width), 1)


def row_iota(rows, width=LANES):
    return lax.broadcasted_iota(jnp.int32, (rows, width), 0)


def halves(rows):
    lane = lane_iota(rows)
    return lane < 64, (lane & 32) == 0


def roll(x, shift):
    return pltpu.roll(x, shift, 1)


def split(x):
    high = x.astype(BF16)
    low = (x - high.astype(F32)).astype(BF16)
    return high, low


def dot(a, b):
    return lax.dot_general(a, b, (((1,), (0,)), ((), ())), preferred_element_type=F32)


def dot_nt(a, b):
    return lax.dot_general(a, b, (((1,), (1,)), ((), ())), preferred_element_type=F32)


def product(left, right):
    high, low = split(right)
    rows = left.shape[0] // 2
    width = right.shape[1]
    wide = dot(left, jnp.concatenate([high, low], axis=1))
    return wide[:rows, :width] + (wide[rows:, :width] + wide[:rows, width:])


def stack_split(x):
    high, low = split(x)
    return jnp.concatenate([high.astype(F32), low.astype(F32)], axis=0).astype(BF16)


def spread(columns):
    first, even = halves(8)
    tiles = []
    for column in columns[:2]:
        turned = roll(column, 64)
        for pair in (jnp.where(first, column, turned), jnp.where(first, turned, column)):
            moved = roll(pair, 32)
            tiles.append(jnp.where(even, pair, moved))
            tiles.append(jnp.where(even, moved, pair))
    pair = jnp.where(first, columns[2], roll(columns[2], 64))
    tiles.append(jnp.where(even, pair, roll(pair, 32)))
    return tiles


def group_swap(parts):
    first, even = halves(8)
    a0, a1, a2, a3 = parts
    out = []
    p = [jnp.where(first, a0, roll(a2, 64)), jnp.where(first, a1, roll(a3, 64))]
    r = [jnp.where(first, roll(a0, 64), a2), jnp.where(first, roll(a1, 64), a3)]
    for x, y in (p, r):
        out.append(jnp.where(even, x, roll(y, 32)))
        out.append(jnp.where(even, roll(x, 96), y))
    return out


def group_place(parts):
    total = parts[0]
    for group, part in enumerate(parts[1:], 1):
        total = total + roll(part, 32 * group)
    return total


def widen(x, pad):
    rows = x.shape[0]
    pad[0:rows, 0:E] = x
    return pad[0:rows, :]


def weigh(rows_of, x_ref, y_ref, count):
    for tile in range(M // 8):
        spans = spread([x_ref[tile * 8 : tile * 8 + 8, c * 128 : c * 128 + 128] for c in range(3)])
        for d in range(count):
            for c in range(3):
                total = rows_of[d * 16 : d * 16 + 1, c * 128 : c * 128 + 128] * spans[0]
                for p in range(1, Q):
                    total = total + rows_of[d * 16 + p : d * 16 + p + 1, c * 128 : c * 128 + 128] * spans[p]
                start = d * M + tile * 8
                y_ref[start : start + 8, c * 128 : c * 128 + 128] = total


def predict(star, left, x_ref, y_ref, first_ref, second_ref):
    y_ref[3 * M : 3 * M + 8, :] = jnp.zeros((8, W), F32)
    state = x_ref[...]
    first_ref[...] = EARLY[0] * state
    if second_ref is not None:
        second_ref[...] = LATE[0] * state

    def step(k, carry):
        weigh(star, x_ref, y_ref, 3)
        result = product(left[...], y_ref[0 : 3 * M + 8, :])
        x_ref[...] = result
        early = jnp.float32(EARLY[1])
        late = jnp.float32(LATE[1])
        for degree in range(2, TERMS):
            early = jnp.where(k == degree, EARLY[degree], early)
            late = jnp.where(k == degree, LATE[degree], late)
        first_ref[...] = first_ref[...] + early * result
        if second_ref is not None:
            second_ref[...] = second_ref[...] + late * result
        return carry

    lax.fori_loop(1, TERMS, step, 0)


def make_table(project, x, tab_ref):
    faced = product(project, x)
    for tile in range(3):
        for c in range(3):
            parts = [
                faced[f * JP + tile * 8 : f * JP + tile * 8 + 8, c * 128 : c * 128 + 128] for f in range(4)
            ]
            swapped = group_swap(parts)
            for g in range(4 if c < 2 else 1):
                row = (c * 4 + g) * JP + tile * 8
                tab_ref[row : row + 8, :] = swapped[g]
    tab_ref[Q * JP : TAB, :] = jnp.zeros((TAB - Q * JP, LANES), F32)


def send_rows(pick, tab_ref):
    high, low = split(tab_ref[...])
    return dot_nt(pick, high) + dot_nt(pick, low)


def off_rank():
    return lax.axis_index("off")


def put_sends(rows, bw_ref, fw_ref, self_ref, off_refs):
    bw_ref[...] = rows[0:16]
    fw_ref[...] = rows[16:32]
    self_ref[...] = rows[32:48]
    for k, ref in enumerate(off_refs):
        ref[...] = rows[48 + 16 * k : 64 + 16 * k]


def first_kernel(n_off, state_in, star_in, stiff_in, proj_in, elem_in, face_in, *refs):
    (state_out, first_out, second_out, star_out, left_out, proj_out, tab_out, pick_out, bw, fw, own) = refs[:11]
    offs = refs[11 : 11 + n_off - 1]
    x_ref, y_ref, pad, high_pad, slot_pad = refs[11 + n_off - 1 :]
    pad[...] = jnp.zeros((64, LANES), F32)
    for c in range(3):
        parts = [widen(state_in[q], pad) for q in range(4 * c, min(4 * c + 4, Q))]
        column = group_place(parts)
        x_ref[:, c * 128 : c * 128 + 128] = column
        state_out[:, c * 128 : c * 128 + 128] = column
    pad[...] = jnp.zeros((64, LANES), F32)
    for d in range(3):
        for c in range(3):
            parts = []
            for q in range(4 * c, min(4 * c + 4, Q)):
                pad[0:Q, 0:E] = star_in[d, q]
                parts.append(pad[0:16, :])
            star_out[d * 16 : d * 16 + 16, c * 128 : c * 128 + 128] = group_place(parts)
    high_pad[...] = jnp.zeros((256, LANES), F32)
    for d in range(3):
        high_pad[d * M : d * M + M, 0:M] = stiff_in[d]
    left_out[...] = stack_split(high_pad[...].T[0:M, 0 : 3 * M + 8])
    high_pad[...] = jnp.zeros((256, LANES), F32)
    for f in range(4):
        high_pad[f * 64 : f * 64 + M, 0:J] = proj_in[f]
    turned = high_pad[...].T
    proj_out[...] = stack_split(
        jnp.concatenate([turned[0:JP, f * 64 : f * 64 + M] for f in range(4)], axis=0)
    )
    slots = elem_in.shape[2]
    slot_pad[...] = jnp.zeros((8, LANES), jnp.int32)
    slot_pad[0:1, 0:slots] = face_in[0] * E + elem_in[0] + 1
    rows = 32 + 16 * n_off
    row = row_iota(rows)
    block = row >> 4
    within = row & 15
    target = lax.rem(block - 2 + off_rank(), n_off)
    slot = jnp.where(row < 32, row, jnp.where(within < SO, 32 + target * SO + within, -1))
    wanted = jnp.where(lane_iota(rows) == slot, slot_pad[0:1, :], 0)
    entry = jnp.sum(wanted.astype(F32), axis=1, keepdims=True)
    pick = jnp.where(lane_iota(rows).astype(F32) + 1.0 == entry, 1.0, 0.0).astype(BF16)
    pick_out[...] = pick

    predict(star_out, left_out, x_ref, y_ref, first_out, second_out)
    make_table(proj_out[...], first_out[...], tab_out)
    put_sends(send_rows(pick, tab_out), bw, fw, own, offs)


def gather_local(pick, tab_ref):
    high, low = split(tab_ref[0 : Q * JP + 8, :])
    return dot(high, pick) + dot(low, pick)


def side_kernel(
    n_off,
    first_in,
    star,
    tab,
    local_in,
    nbr_in,
    vol_in,
    minus_in,
    turn_in,
    lift_in,
    index_in,
    orient_in,
    cluster_in,
    source_elem,
    source_in,
    part_out,
    coef_out,
    fnbr_out,
    left_out,
    lift_out,
    here_out,
    pick_here_out,
    pick_far_out,
    flags_out,
    source_out,
    y_ref,
    pad,
    tall,
    turn_pad,
    lift_pad,
    ipad,
):
    pad[...] = jnp.zeros((64, LANES), F32)
    for d in range(3):
        coef_out[d * 16 : d * 16 + 16, :] = star[d * 16 : d * 16 + 16, :]
    for f in range(4):
        for c in range(3):
            parts = []
            for q in range(4 * c, min(4 * c + 4, Q)):
                pad[0:Q, 0:E] = local_in[f, q]
                parts.append(pad[0:16, :])
            coef_out[(3 + f) * 16 : (4 + f) * 16, c * 128 : c * 128 + 128] = group_place(parts)
    for q in range(Q):
        parts = []
        for f in range(4):
            pad[0:Q, 0:E] = nbr_in[f, q]
            parts.append(pad[0:16, :])
        fnbr_out[q * 16 : q * 16 + 16, :] = group_place(parts)
    tall[...] = jnp.zeros((512, LANES), F32)
    for d in range(3):
        tall[d * M : d * M + M, 0:M] = vol_in[d]
    for f in range(4):
        tall[(3 + f) * M : (4 + f) * M, 0:M] = minus_in[f]
    left_out[...] = stack_split(tall[...].T[0:M, 0 : 7 * M + 8])
    turn_pad[...] = jnp.zeros((3 * JP, LANES), F32)
    for o in range(3):
        turn_pad[o * JP : o * JP + J, 0:J] = turn_in[o]
    tall[...] = jnp.zeros((512, LANES), F32)
    lift_pad[...] = jnp.zeros((LANES, LANES), F32)
    for f in range(4):
        lift_pad[0:J, 0:M] = lift_in[f]
        tall[f * 3 * JP : (f + 1) * 3 * JP, :] = lax.dot_general(
            turn_pad[...],
            lift_pad[...],
            (((1,), (0,)), ((), ())),
            precision=lax.Precision.HIGHEST,
            preferred_element_type=F32,
        )
    lift_out[...] = stack_split(tall[...].T[0:M, 0 : 12 * JP])
    ipad[...] = jnp.zeros((8, LANES), jnp.int32)
    ipad[0:4, 0:E] = index_in[...]
    index_row = group_place([ipad[f : f + 1, :] for f in range(4)])
    ipad[0:4, 0:E] = orient_in[...]
    ipad[4:5, 0:E] = cluster_in[...]
    orient = ipad[...]
    twice = orient + roll(orient, 64)
    flags_out[...] = twice + roll(twice, 32)
    pick_here = jnp.where(row_iota(LANES) == index_row, 1.0, 0.0).astype(BF16)
    pick_here_out[...] = pick_here
    rows = 32 + 16 * n_off
    row = row_iota(rows)
    within = row & 15
    source = lax.rem(off_rank() + n_off + 2 - (row >> 4), n_off)
    place = jnp.where(
        row < 32, LANES + row, jnp.where(within < SO, LANES + 32 + source * SO + within, -1)
    )
    pick_far_out[...] = jnp.where(place == index_row, 1.0, 0.0).astype(BF16)
    here_out[...] = gather_local(pick_here, tab)
    tall[...] = jnp.zeros((512, LANES), F32)
    for s in range(SRC):
        tall[s * 16 : s * 16 + Q, 0:M] = source_in[s]
    origin = (lax.axis_index("fault") * n_off + off_rank()) * E
    row16 = row_iota(16, W)
    lane16 = lane_iota(16, W)
    for s in range(SRC):
        spot = source_elem[s] - origin
        inside = jnp.logical_and(spot >= 0, spot < E)
        goal = jnp.where(inside, spot, -100000)
        y_ref[s * 16 : s * 16 + 16, :] = jnp.where(
            jnp.logical_and(lane16 == row16 * E + goal, row16 < Q), 1.0, 0.0
        )
    picks = y_ref[0 : SRC * 16, :].astype(BF16)
    high, low = split(tall[...].T[0:M, 0 : SRC * 16])
    rest = tall[...].T[0:M, 0 : SRC * 16] - high.astype(F32) - low.astype(F32)
    source_out[...] = dot(high, picks) + (dot(low, picks) + dot(rest.astype(BF16), picks))

    weigh(coef_out, first_in, y_ref, 7)
    y_ref[7 * M : 7 * M + 8, :] = jnp.zeros((8, W), F32)
    part_out[...] = product(left_out[...], y_ref[...])


def arrive(n_off, fw, bw, own, offs, pick_far, stage):
    stage[0:16, :] = fw[...]
    stage[16:32, :] = bw[...]
    stage[32:48, :] = own[...]
    for k, ref in enumerate(offs):
        stage[48 + 16 * k : 64 + 16 * k, :] = ref[...]
    turned = stage[...].T[0 : Q * JP + 8, :]
    high, low = split(turned)
    return dot(high, pick_far[...]) + dot(low, pick_far[...])


def neighbour_flux(near_ref, fnbr, flags, lift, y_ref):
    for tile in range(3):
        near = [near_ref[p * JP + tile * 8 : p * JP + tile * 8 + 8, :] for p in range(Q)]
        fluxes = []
        for q in range(Q):
            total = fnbr[q * 16 : q * 16 + 1, :] * near[0]
            for p in range(1, Q):
                total = total + fnbr[q * 16 + p : q * 16 + p + 1, :] * near[p]
            fluxes.append(total)
        zero = jnp.zeros((8, LANES), F32)
        for c in range(3):
            parts = [fluxes[4 * c + g] if 4 * c + g < Q else zero for g in range(4)]
            swapped = group_swap(parts)
            for f in range(4):
                facing = flags[f : f + 1, :]
                for o in range(3):
                    start = (f * 3 + o) * JP + tile * 8
                    y_ref[start : start + 8, c * 128 : c * 128 + 128] = jnp.where(
                        facing == o, swapped[f], 0.0
                    )
    return product(lift[...], y_ref[0 : 12 * JP, :])


def wide_fine(flags):
    row = flags[4:5, :] == 1
    return row


def middle_kernel(
    n_off, state, second, part, here, fnbr, flags, lift, star, left, proj, pick, pick_far, own, fw, bw, *refs
):
    offs = refs[: n_off - 1]
    outs = refs[n_off - 1 :]
    near_out, half_out, later_out, tab_out, bw_out, fw_out, own_out = outs[:7]
    off_outs = outs[7 : 7 + n_off - 1]
    x_ref, y_ref, stage, acc = outs[7 + n_off - 1 :]
    near_out[...] = here[...] + arrive(n_off, fw, bw, own, offs, pick_far, stage)
    total = part[...] + neighbour_flux(near_out, fnbr, flags, lift, y_ref)
    fine = jnp.concatenate([wide_fine(flags)] * 3, axis=1)
    base = state[...]
    half = jnp.where(fine, base + total, base)
    half_out[...] = half
    x_ref[...] = half
    predict(star, left, x_ref, y_ref, acc, None)
    later = jnp.where(fine, acc[...], second[...])
    later_out[...] = later
    make_table(proj[...], later, tab_out)
    put_sends(send_rows(pick[...], tab_out), bw_out, fw_out, own_out, off_outs)


def late_side_kernel(
    first, second, later, half, source, near_first, tab, coef, left, flags, pick_here, base_out, here_out, x_ref, y_ref
):
    row = wide_fine(flags)
    fine = jnp.concatenate([row] * 3, axis=1)
    x_ref[...] = jnp.where(fine, later[...], first[...] + second[...])
    weigh(coef, x_ref, y_ref, 7)
    y_ref[7 * M : 7 * M + 8, :] = jnp.zeros((8, W), F32)
    base_out[...] = half[...] + source[...] + product(left[...], y_ref[...])
    here_out[...] = gather_local(pick_here[...], tab) + jnp.where(row, 0.0, near_first[...])


def last_kernel(n_off, base, here, fnbr, flags, lift, pick_far, own, fw, bw, *refs):
    offs = refs[: n_off - 1]
    out, near, y_ref, stage = refs[n_off - 1 :]
    near[...] = here[...] + arrive(n_off, fw, bw, own, offs, pick_far, stage)
    total = base[...] + neighbour_flux(near, fnbr, flags, lift, y_ref)
    for q in range(Q):
        column = total[:, (q // 4) * 128 : (q // 4) * 128 + 128]
        if q % 4:
            column = roll(column, 128 - 32 * (q % 4))
        out[q] = column[:, 0:E]


def shape(*dims, dtype=F32):
    return jax.ShapeDtypeStruct(dims, dtype)


def call(kernel, ins, outs, scratch, name, smem=(), cost=2000000):
    specs = [
        pl.BlockSpec(memory_space=pltpu.SMEM if k in smem else pltpu.VMEM) for k in range(len(ins))
    ]
    return pl.pallas_call(
        kernel,
        in_specs=specs,
        out_specs=[pl.BlockSpec(memory_space=pltpu.VMEM)] * len(outs),
        out_shape=outs,
        scratch_shapes=scratch,
        name=name,
        compiler_params=pltpu.CompilerParams(vmem_limit_bytes=16 * 1024 * 1024),
        cost_estimate=pl.CostEstimate(flops=cost * 1000, bytes_accessed=cost, transcendentals=0),
    )(*ins)


def trade(bw, fw, offs, n_fault, n_off):
    up = [(i, (i + 1) % n_fault) for i in range(n_fault)]
    down = [((i + 1) % n_fault, i) for i in range(n_fault)]
    got = []
    for k, rows in enumerate(offs, 1):
        got.append(lax.ppermute(rows, "off", [(j, (j + k) % n_off) for j in range(n_off)]))
    return lax.ppermute(fw, "fault", up), lax.ppermute(bw, "fault", down), got


def on_device(
    n_fault,
    n_off,
    modal_state,
    star_mats,
    flux_local,
    flux_nbr,
    stiff_time,
    stiff_vol,
    flux_minus,
    face_proj,
    face_turn,
    face_lift,
    cluster,
    send_elem,
    send_face,
    nbr_index,
    orientation,
    source_elem,
    source_term,
):
    vmem = pltpu.VMEM
    rows = 32 + 16 * n_off
    wide = shape(M, W)
    table = shape(TAB, LANES)
    block = shape(16, TAB)
    near = shape(Q * JP + 8, LANES)
    outs = call(
        functools.partial(first_kernel, n_off),
        (modal_state, star_mats, stiff_time, face_proj, send_elem, send_face),
        [
            wide,
            wide,
            wide,
            shape(48, W),
            shape(2 * M, 3 * M + 8, dtype=BF16),
            shape(8 * JP, M, dtype=BF16),
            table,
            shape(rows, LANES, dtype=BF16),
        ]
        + [block] * (3 + n_off - 1),
        [
            vmem((M, W), F32),
            vmem((3 * M + 8, W), F32),
            vmem((64, LANES), F32),
            vmem((256, LANES), F32),
            vmem((8, LANES), jnp.int32),
        ],
        "first",
    )
    state, first, second, star, left, proj, tab, pick, bw, fw, own = outs[:11]
    got_fw, got_bw, got_off = trade(bw, fw, outs[11:], n_fault, n_off)
    part, coef, fnbr, left_all, lift, here, pick_here, pick_far, flags, source = call(
        functools.partial(side_kernel, n_off),
        (
            first,
            star,
            tab,
            flux_local,
            flux_nbr,
            stiff_vol,
            flux_minus,
            face_turn,
            face_lift,
            nbr_index,
            orientation,
            cluster.reshape(1, E),
            source_elem,
            source_term,
        ),
        [
            wide,
            shape(7 * 16, W),
            shape(Q * 16, LANES),
            shape(2 * M, 7 * M + 8, dtype=BF16),
            shape(2 * M, 12 * JP, dtype=BF16),
            near,
            shape(LANES, LANES, dtype=BF16),
            shape(rows, LANES, dtype=BF16),
            shape(8, LANES, dtype=jnp.int32),
            wide,
        ],
        [
            vmem((7 * M + 8, W), F32),
            vmem((64, LANES), F32),
            vmem((512, LANES), F32),
            vmem((3 * JP, LANES), F32),
            vmem((LANES, LANES), F32),
            vmem((8, LANES), jnp.int32),
        ],
        "side",
        smem=(12,),
    )
    outs = call(
        functools.partial(middle_kernel, n_off),
        (state, second, part, here, fnbr, flags, lift, star, left, proj, pick, pick_far, own, got_fw, got_bw, *got_off),
        [near, wide, wide, table] + [block] * (3 + n_off - 1),
        [vmem((M, W), F32), vmem((12 * JP, W), F32), vmem((rows, TAB), F32), vmem((M, W), F32)],
        "middle",
    )
    near_first, half, later, tab, bw, fw, own = outs[:7]
    got_fw, got_bw, got_off = trade(bw, fw, outs[7:], n_fault, n_off)
    base, here = call(
        late_side_kernel,
        (first, second, later, half, source, near_first, tab, coef, left_all, flags, pick_here),
        [wide, near],
        [vmem((M, W), F32), vmem((7 * M + 8, W), F32)],
        "late_side",
    )
    (result,) = call(
        functools.partial(last_kernel, n_off),
        (base, here, fnbr, flags, lift, pick_far, own, got_fw, got_bw, *got_off),
        [shape(Q, M, E)],
        [vmem((Q * JP + 8, LANES), F32), vmem((12 * JP, W), F32), vmem((rows, TAB), F32)],
        "last",
    )
    return result


def solution(mesh):
    n_fault, n_off = mesh.shape["fault"], mesh.shape["off"]
    both = ("fault", "off")
    in_specs = (
        P(None, None, both),
        P(None, None, None, both),
        P(None, None, None, both),
        P(None, None, None, both),
        P(),
        P(),
        P(),
        P(),
        P(),
        P(),
        P(both),
        P("fault", "off", None),
        P("fault", "off", None),
        P(None, both),
        P(None, both),
        P(),
        P(),
    )
    return jax.shard_map(
        functools.partial(on_device, n_fault, n_off),
        mesh=mesh,
        in_specs=in_specs,
        out_specs=P(None, None, both),
        check_vma=False,
    )
```

```python
import functools
import math

import jax
import jax.numpy as jnp
from jax import lax
from jax.experimental import pallas as pl
from jax.experimental.pallas import tpu as pltpu
from jax.sharding import PartitionSpec as P


Q = 9
M = 56
J = 21
JP = 24
E = 32
LANES = 128
W = 384
SO = 10
SRC = 16
TERMS = 6
EARLY = [0.5 ** (k + 1) / math.factorial(k + 1) for k in range(TERMS)]
LATE = [(1.0 - 0.5 ** (k + 1)) / math.factorial(k + 1) for k in range(TERMS)]
F32 = jnp.float32
BF16 = jnp.bfloat16
TAB = 256


def lane_iota(rows, width=LANES):
    return lax.broadcasted_iota(jnp.int32, (rows, width), 1)


def row_iota(rows, width=LANES):
    return lax.broadcasted_iota(jnp.int32, (rows, width), 0)


def halves(rows):
    lane = lane_iota(rows)
    return lane < 64, (lane & 32) == 0


def roll(x, shift):
    return pltpu.roll(x, shift, 1)


def split(x):
    high = x.astype(BF16)
    low = (x - high.astype(F32)).astype(BF16)
    return high, low


def dot(a, b):
    return lax.dot_general(a, b, (((1,), (0,)), ((), ())), preferred_element_type=F32)


def dot_nt(a, b):
    return lax.dot_general(a, b, (((1,), (1,)), ((), ())), preferred_element_type=F32)


def product(left, right):
    high, low = split(right)
    rows = left.shape[0] // 2
    width = right.shape[1]
    wide = dot(left, jnp.concatenate([high, low], axis=1))
    return wide[:rows, :width] + (wide[rows:, :width] + wide[:rows, width:])


def stack_split(x):
    high, low = split(x)
    return jnp.concatenate([high.astype(F32), low.astype(F32)], axis=0).astype(BF16)


def spread(columns):
    first, even = halves(8)
    tiles = []
    for column in columns[:2]:
        turned = roll(column, 64)
        for pair in (jnp.where(first, column, turned), jnp.where(first, turned, column)):
            moved = roll(pair, 32)
            tiles.append(jnp.where(even, pair, moved))
            tiles.append(jnp.where(even, moved, pair))
    pair = jnp.where(first, columns[2], roll(columns[2], 64))
    tiles.append(jnp.where(even, pair, roll(pair, 32)))
    return tiles


def group_swap(parts):
    first, even = halves(8)
    a0, a1, a2, a3 = parts
    out = []
    p = [jnp.where(first, a0, roll(a2, 64)), jnp.where(first, a1, roll(a3, 64))]
    r = [jnp.where(first, roll(a0, 64), a2), jnp.where(first, roll(a1, 64), a3)]
    for x, y in (p, r):
        out.append(jnp.where(even, x, roll(y, 32)))
        out.append(jnp.where(even, roll(x, 96), y))
    return out


def group_place(parts):
    if len(parts) < 4:
        parts = parts + [jnp.zeros((parts[0].shape[0], E * (4 - len(parts))), parts[0].dtype)]
    return jnp.concatenate(parts, axis=1)


def weigh(rows_of, x_ref, y_ref, count):
    for tile in range(M // 8):
        spans = spread([x_ref[tile * 8 : tile * 8 + 8, c * 128 : c * 128 + 128] for c in range(3)])
        for d in range(count):
            for c in range(3):
                total = rows_of[d * 16 : d * 16 + 1, c * 128 : c * 128 + 128] * spans[0]
                for p in range(1, Q):
                    total = total + rows_of[d * 16 + p : d * 16 + p + 1, c * 128 : c * 128 + 128] * spans[p]
                start = d * M + tile * 8
                y_ref[start : start + 8, c * 128 : c * 128 + 128] = total


def predict(star, left, x_ref, y_ref, first_ref, second_ref):
    y_ref[3 * M : 3 * M + 8, :] = jnp.zeros((8, W), F32)
    state = x_ref[...]
    first_ref[...] = EARLY[0] * state
    if second_ref is not None:
        second_ref[...] = LATE[0] * state

    def step(k, carry):
        weigh(star, x_ref, y_ref, 3)
        result = product(left[...], y_ref[0 : 3 * M + 8, :])
        x_ref[...] = result
        early = jnp.float32(EARLY[1])
        late = jnp.float32(LATE[1])
        for degree in range(2, TERMS):
            early = jnp.where(k == degree, EARLY[degree], early)
            late = jnp.where(k == degree, LATE[degree], late)
        first_ref[...] = first_ref[...] + early * result
        if second_ref is not None:
            second_ref[...] = second_ref[...] + late * result
        return carry

    lax.fori_loop(1, TERMS, step, 0)


def make_table(project, x, tab_ref):
    faced = product(project, x)
    for tile in range(3):
        for c in range(3):
            parts = [
                faced[f * JP + tile * 8 : f * JP + tile * 8 + 8, c * 128 : c * 128 + 128] for f in range(4)
            ]
            swapped = group_swap(parts)
            for g in range(4 if c < 2 else 1):
                row = (c * 4 + g) * JP + tile * 8
                tab_ref[row : row + 8, :] = swapped[g]
    tab_ref[Q * JP : TAB, :] = jnp.zeros((TAB - Q * JP, LANES), F32)


def send_rows(pick, tab_ref):
    high, low = split(tab_ref[...])
    return dot_nt(pick, high) + dot_nt(pick, low)


def off_rank():
    return lax.axis_index("off")


def put_sends(rows, bw_ref, fw_ref, self_ref, off_refs):
    bw_ref[...] = rows[0:16]
    fw_ref[...] = rows[16:32]
    self_ref[...] = rows[32:48]
    for k, ref in enumerate(off_refs):
        ref[...] = rows[48 + 16 * k : 64 + 16 * k]


def first_kernel(n_off, *refs):
    sources = refs[:6]
    landed = refs[-7:-1]
    copies = [
        pltpu.make_async_copy(source, target, refs[-1].at[k])
        for k, (source, target) in enumerate(zip(sources, landed))
    ]
    for copy in copies:
        copy.start()
    state_in, star_in, stiff_in, proj_in, elem_in, face_in = landed
    refs = refs[6:-7]
    (state_out, first_out, second_out, star_out, left_out, proj_out, tab_out, pick_out, bw, fw, own) = refs[:11]
    offs = refs[11 : 11 + n_off - 1]
    x_ref, y_ref, tall, slot_pad = refs[11 + n_off - 1 :]
    tall[...] = jnp.zeros((W, LANES), F32)
    slot_pad[...] = jnp.zeros((8, LANES), jnp.int32)
    for copy in copies:
        copy.wait()
    for q in range(Q):
        tall[q * E : q * E + E, 0:M] = state_in[q]
    state = tall[...].T[0:M, :]
    x_ref[...] = state
    state_out[...] = state
    for d in range(3):
        for c in range(3):
            star_out[d * 16 : d * 16 + Q, c * 128 : c * 128 + 128] = group_place(
                [star_in[q, :, d, :] for q in range(4 * c, min(4 * c + 4, Q))]
            )
    tall[...] = jnp.zeros((W, LANES), F32)
    for d in range(3):
        tall[d * M : d * M + M, 0:M] = stiff_in[d]
    left_out[...] = stack_split(tall[0:256, :].T[0:M, 0 : 3 * M + 8])
    tall[0 : 4 * JP, :] = jnp.zeros((4 * JP, LANES), F32)
    for f in range(4):
        tall[f * JP : f * JP + J, 0:M] = proj_in[:, f, :]
    proj_out[...] = stack_split(tall[0 : 4 * JP, 0:M])
    slots = elem_in.shape[2]
    slot_pad[0:1, 0:slots] = face_in[0] * E + elem_in[0] + 1
    rows = 32 + 16 * n_off
    row = row_iota(rows)
    block = row >> 4
    within = row & 15
    target = lax.rem(block - 2 + off_rank(), n_off)
    slot = jnp.where(row < 32, row, jnp.where(within < SO, 32 + target * SO + within, -1))
    wanted = jnp.where(lane_iota(rows) == slot, slot_pad[0:1, :], 0)
    entry = jnp.sum(wanted.astype(F32), axis=1, keepdims=True)
    pick = jnp.where(lane_iota(rows).astype(F32) + 1.0 == entry, 1.0, 0.0).astype(BF16)
    pick_out[...] = pick

    predict(star_out, left_out, x_ref, y_ref, first_out, second_out)
    make_table(proj_out[...], first_out[...], tab_out)
    put_sends(send_rows(pick, tab_out), bw, fw, own, offs)


def gather_local(pick, tab_ref):
    high, low = split(tab_ref[0 : Q * JP + 8, :])
    return dot(high, pick) + dot(low, pick)


def side_kernel(
    n_off,
    first_in,
    star,
    tab,
    local_in,
    nbr_in,
    vol_in,
    minus_in,
    turn_in,
    lift_in,
    index_in,
    orient_in,
    cluster_in,
    source_elem,
    source_in,
    part_out,
    coef_out,
    fnbr_out,
    left_out,
    lift_out,
    here_out,
    pick_here_out,
    pick_far_out,
    flags_out,
    source_out,
    y_ref,
    tall,
    turn_pad,
    lift_pad,
    ipad,
):
    coef_out[0:48, :] = star[...]
    for f in range(4):
        for c in range(3):
            coef_out[(3 + f) * 16 : (3 + f) * 16 + Q, c * 128 : c * 128 + 128] = group_place(
                [local_in[q, :, f, :] for q in range(4 * c, min(4 * c + 4, Q))]
            )
    for q in range(Q):
        fnbr_out[q * 16 : q * 16 + Q, :] = group_place([nbr_in[q, :, f, :] for f in range(4)])
    tall[...] = jnp.zeros((512, LANES), F32)
    for d in range(3):
        tall[d * M : d * M + M, 0:M] = vol_in[d]
    for f in range(4):
        tall[(3 + f) * M : (4 + f) * M, 0:M] = minus_in[f]
    left_out[...] = stack_split(tall[...].T[0:M, 0 : 7 * M + 8])
    turn_pad[...] = jnp.zeros((3 * JP, LANES), F32)
    for o in range(3):
        turn_pad[o * JP : o * JP + J, 0:J] = turn_in[o]
    tall[...] = jnp.zeros((512, LANES), F32)
    lift_pad[...] = jnp.zeros((LANES, LANES), F32)
    for f in range(4):
        lift_pad[0:J, 0:M] = lift_in[:, f, :]
        tall[f * 3 * JP : (f + 1) * 3 * JP, :] = lax.dot_general(
            turn_pad[...],
            lift_pad[...],
            (((1,), (0,)), ((), ())),
            precision=lax.Precision.HIGHEST,
            preferred_element_type=F32,
        )
    lift_out[...] = stack_split(tall[...].T[0:M, 0 : 12 * JP])
    ipad[...] = jnp.zeros((8, LANES), jnp.int32)
    index_row = group_place([index_in[f : f + 1, :] for f in range(4)])
    ipad[0:4, 0:E] = orient_in[...]
    ipad[4:5, 0:E] = cluster_in[...]
    orient = ipad[...]
    twice = orient + roll(orient, 64)
    flags_out[...] = twice + roll(twice, 32)
    pick_here = jnp.where(row_iota(LANES) == index_row, 1.0, 0.0).astype(BF16)
    pick_here_out[...] = pick_here
    rows = 32 + 16 * n_off
    row = row_iota(rows)
    within = row & 15
    source = lax.rem(off_rank() + n_off + 2 - (row >> 4), n_off)
    place = jnp.where(
        row < 32, LANES + row, jnp.where(within < SO, LANES + 32 + source * SO + within, -1)
    )
    pick_far_out[...] = jnp.where(place == index_row, 1.0, 0.0).astype(BF16)
    here_out[...] = gather_local(pick_here, tab)
    tall[...] = jnp.zeros((512, LANES), F32)
    for q in range(Q):
        tall[q * SRC : q * SRC + SRC, 0:M] = source_in[q]
    origin = (lax.axis_index("fault") * n_off + off_rank()) * E
    row = row_iota(SRC)
    goal = jnp.full((SRC, LANES), -1, jnp.int32)
    for s in range(SRC):
        goal = jnp.where(row == s, source_elem[s] - origin, goal)
    y_ref[0 : Q * SRC, :] = jnp.zeros((Q * SRC, W), F32)
    lane = lane_iota(SRC)
    for q in range(Q):
        lane_in = lane - 32 * (q % 4)
        hit = jnp.logical_and(lane_in == goal, jnp.logical_and(goal >= 0, goal < E))
        c = q // 4
        y_ref[q * SRC : q * SRC + SRC, c * 128 : c * 128 + 128] = jnp.where(hit, 1.0, 0.0)
    picks = y_ref[0 : Q * SRC, :].astype(BF16)
    terms = tall[0:256, :].T[0:M, 0 : Q * SRC]
    high, low = split(terms)
    rest = (terms - high.astype(F32) - low.astype(F32)).astype(BF16)
    source_out[...] = dot(high, picks) + (dot(low, picks) + dot(rest, picks))

    weigh(coef_out, first_in, y_ref, 7)
    y_ref[7 * M : 7 * M + 8, :] = jnp.zeros((8, W), F32)
    part_out[...] = product(left_out[...], y_ref[...])


def arrive(fw, bw, own, offs, pick_far, stage):
    stage[0:16, :] = fw[...]
    stage[16:32, :] = bw[...]
    stage[32:48, :] = own[...]
    for k, ref in enumerate(offs):
        stage[48 + 16 * k : 64 + 16 * k, :] = ref[...]
    turned = stage[...].T[0 : Q * JP + 8, :]
    high, low = split(turned)
    return dot(high, pick_far[...]) + dot(low, pick_far[...])


def neighbour_flux(near_ref, fnbr, flags, lift, y_ref):
    for tile in range(3):
        near = [near_ref[p * JP + tile * 8 : p * JP + tile * 8 + 8, :] for p in range(Q)]
        fluxes = []
        for q in range(Q):
            total = fnbr[q * 16 : q * 16 + 1, :] * near[0]
            for p in range(1, Q):
                total = total + fnbr[q * 16 + p : q * 16 + p + 1, :] * near[p]
            fluxes.append(total)
        zero = jnp.zeros((8, LANES), F32)
        for c in range(3):
            parts = [fluxes[4 * c + g] if 4 * c + g < Q else zero for g in range(4)]
            swapped = group_swap(parts)
            for f in range(4):
                facing = flags[f : f + 1, :]
                for o in range(3):
                    start = (f * 3 + o) * JP + tile * 8
                    y_ref[start : start + 8, c * 128 : c * 128 + 128] = jnp.where(
                        facing == o, swapped[f], 0.0
                    )
    return product(lift[...], y_ref[0 : 12 * JP, :])


def wide_fine(flags):
    row = flags[4:5, :] == 1
    return row


def middle_kernel(
    n_off, state, second, part, here, fnbr, flags, lift, star, left, proj, pick, pick_far, own, fw, bw, *refs
):
    offs = refs[: n_off - 1]
    outs = refs[n_off - 1 :]
    near_out, half_out, later_out, tab_out, bw_out, fw_out, own_out = outs[:7]
    off_outs = outs[7 : 7 + n_off - 1]
    x_ref, y_ref, stage, acc = outs[7 + n_off - 1 :]
    near_out[...] = here[...] + arrive(fw, bw, own, offs, pick_far, stage)
    total = part[...] + neighbour_flux(near_out, fnbr, flags, lift, y_ref)
    fine = jnp.concatenate([wide_fine(flags)] * 3, axis=1)
    base = state[...]
    half = jnp.where(fine, base + total, base)
    half_out[...] = half
    x_ref[...] = half
    predict(star, left, x_ref, y_ref, acc, None)
    later = jnp.where(fine, acc[...], second[...])
    later_out[...] = later
    make_table(proj[...], later, tab_out)
    put_sends(send_rows(pick[...], tab_out), bw_out, fw_out, own_out, off_outs)


def late_side_kernel(
    first, second, later, half, source, near_first, tab, coef, left, flags, pick_here, base_out, here_out, x_ref, y_ref
):
    row = wide_fine(flags)
    fine = jnp.concatenate([row] * 3, axis=1)
    x_ref[...] = jnp.where(fine, later[...], first[...] + second[...])
    weigh(coef, x_ref, y_ref, 7)
    y_ref[7 * M : 7 * M + 8, :] = jnp.zeros((8, W), F32)
    base_out[...] = half[...] + source[...] + product(left[...], y_ref[...])
    here_out[...] = gather_local(pick_here[...], tab) + jnp.where(row, 0.0, near_first[...])


def last_kernel(n_off, base, here, fnbr, flags, lift, pick_far, own, fw, bw, *refs):
    offs = refs[: n_off - 1]
    out, near, y_ref, stage, tall = refs[n_off - 1 :]
    tall[M:LANES, :] = jnp.zeros((LANES - M, W), F32)
    near[...] = here[...] + arrive(fw, bw, own, offs, pick_far, stage)
    total = base[...] + neighbour_flux(near, fnbr, flags, lift, y_ref)
    tall[0:M, :] = total
    turned = tall[...].T
    for q in range(Q):
        out[q] = turned[q * E : q * E + E, 0:M]


def shape(*dims, dtype=F32):
    return jax.ShapeDtypeStruct(dims, dtype)


def call(kernel, ins, outs, scratch, smem=(), hbm=(), cost=2000000):
    specs = [
        pl.BlockSpec(
            memory_space=pltpu.SMEM if k in smem else pltpu.HBM if k in hbm else pltpu.VMEM
        )
        for k in range(len(ins))
    ]
    return pl.pallas_call(
        kernel,
        in_specs=specs,
        out_specs=[pl.BlockSpec(memory_space=pltpu.VMEM)] * len(outs),
        out_shape=outs,
        scratch_shapes=scratch,
        compiler_params=pltpu.CompilerParams(vmem_limit_bytes=16 * 1024 * 1024),
        cost_estimate=pl.CostEstimate(flops=cost * 1000, bytes_accessed=cost, transcendentals=0),
    )(*ins)


def trade(bw, fw, offs, n_fault, n_off):
    up = [(i, (i + 1) % n_fault) for i in range(n_fault)]
    down = [((i + 1) % n_fault, i) for i in range(n_fault)]
    got = []
    for k, rows in enumerate(offs, 1):
        got.append(lax.ppermute(rows, "off", [(j, (j + k) % n_off) for j in range(n_off)]))
    ahead = lax.ppermute(fw, "fault", up)
    behind = lax.ppermute(bw, "fault", down)
    return ahead, behind, got


def on_device(
    n_fault,
    n_off,
    modal_state,
    star_mats,
    flux_local,
    flux_nbr,
    stiff_time,
    stiff_vol,
    flux_minus,
    face_proj,
    face_turn,
    face_lift,
    cluster,
    send_elem,
    send_face,
    nbr_index,
    orientation,
    source_elem,
    source_term,
):
    vmem = pltpu.VMEM
    rows = 32 + 16 * n_off
    wide = shape(M, W)
    table = shape(TAB, LANES)
    block = shape(16, TAB)
    near = shape(Q * JP + 8, LANES)
    given = (
        jnp.transpose(modal_state, (0, 2, 1)),
        jnp.transpose(star_mats, (1, 2, 0, 3)),
        stiff_time,
        jnp.transpose(face_proj, (2, 0, 1)),
        send_elem,
        send_face,
    )
    outs = call(
        functools.partial(first_kernel, n_off),
        [pltpu.with_memory_space_constraint(x, pltpu.HBM) for x in given],
        [
            wide,
            wide,
            wide,
            shape(48, W),
            shape(2 * M, 3 * M + 8, dtype=BF16),
            shape(8 * JP, M, dtype=BF16),
            table,
            shape(rows, LANES, dtype=BF16),
        ]
        + [block] * (3 + n_off - 1),
        [
            vmem((M, W), F32),
            vmem((3 * M + 8, W), F32),
            vmem((W, LANES), F32),
            vmem((8, LANES), jnp.int32),
        ]
        + [vmem(x.shape, x.dtype) for x in given]
        + [pltpu.SemaphoreType.DMA((len(given),))],
        hbm=range(len(given)),
    )
    state, first, second, star, left, proj, tab, pick, bw, fw, own = outs[:11]
    got_fw, got_bw, got_off = trade(bw, fw, outs[11:], n_fault, n_off)
    part, coef, fnbr, left_all, lift, here, pick_here, pick_far, flags, source = call(
        functools.partial(side_kernel, n_off),
        (
            first,
            star,
            tab,
            jnp.transpose(flux_local, (1, 2, 0, 3)),
            jnp.transpose(flux_nbr, (1, 2, 0, 3)),
            stiff_vol,
            flux_minus,
            face_turn,
            jnp.transpose(face_lift, (1, 0, 2)),
            nbr_index,
            orientation,
            cluster.reshape(1, E),
            source_elem,
            jnp.transpose(source_term, (1, 0, 2)),
        ),
        [
            wide,
            shape(7 * 16, W),
            shape(Q * 16, LANES),
            shape(2 * M, 7 * M + 8, dtype=BF16),
            shape(2 * M, 12 * JP, dtype=BF16),
            near,
            shape(LANES, LANES, dtype=BF16),
            shape(rows, LANES, dtype=BF16),
            shape(8, LANES, dtype=jnp.int32),
            wide,
        ],
        [
            vmem((7 * M + 8, W), F32),
            vmem((512, LANES), F32),
            vmem((3 * JP, LANES), F32),
            vmem((LANES, LANES), F32),
            vmem((8, LANES), jnp.int32),
        ],
        smem=(12,),
    )
    outs = call(
        functools.partial(middle_kernel, n_off),
        (state, second, part, here, fnbr, flags, lift, star, left, proj, pick, pick_far, own, got_fw, got_bw, *got_off),
        [near, wide, wide, table] + [block] * (3 + n_off - 1),
        [vmem((M, W), F32), vmem((12 * JP, W), F32), vmem((rows, TAB), F32), vmem((M, W), F32)],
    )
    near_first, half, later, tab, bw, fw, own = outs[:7]
    got_fw, got_bw, got_off = trade(bw, fw, outs[7:], n_fault, n_off)
    base, here = call(
        late_side_kernel,
        (first, second, later, half, source, near_first, tab, coef, left_all, flags, pick_here),
        [wide, near],
        [vmem((M, W), F32), vmem((7 * M + 8, W), F32)],
    )
    (result,) = call(
        functools.partial(last_kernel, n_off),
        (base, here, fnbr, flags, lift, pick_far, own, got_fw, got_bw, *got_off),
        [shape(Q, E, M)],
        [vmem((Q * JP + 8, LANES), F32), vmem((12 * JP, W), F32), vmem((rows, TAB), F32), vmem((LANES, W), F32)],
    )
    return jnp.transpose(result, (0, 2, 1))


def solution(mesh):
    n_fault, n_off = mesh.shape["fault"], mesh.shape["off"]
    both = ("fault", "off")
    in_specs = (
        P(None, None, both),
        P(None, None, None, both),
        P(None, None, None, both),
        P(None, None, None, both),
        P(),
        P(),
        P(),
        P(),
        P(),
        P(),
        P(both),
        P("fault", "off", None),
        P("fault", "off", None),
        P(None, both),
        P(None, both),
        P(),
        P(),
    )
    return jax.shard_map(
        functools.partial(on_device, n_fault, n_off),
        mesh=mesh,
        in_specs=in_specs,
        out_specs=P(None, None, both),
        check_vma=False,
    )
```

```python
import functools
import math

import jax
import jax.numpy as jnp
from jax import lax
from jax.experimental import pallas as pl
from jax.experimental.pallas import tpu as pltpu
from jax.sharding import PartitionSpec as P


Q = 9
M = 56
J = 21
JP = 24
E = 32
LANES = 128
W = 384
SO = 10
SRC = 16
TERMS = 6
EARLY = [0.5 ** (k + 1) / math.factorial(k + 1) for k in range(TERMS)]
LATE = [(1.0 - 0.5 ** (k + 1)) / math.factorial(k + 1) for k in range(TERMS)]
F32 = jnp.float32
BF16 = jnp.bfloat16
TAB = 256


def lane_iota(rows, width=LANES):
    return lax.broadcasted_iota(jnp.int32, (rows, width), 1)


def row_iota(rows, width=LANES):
    return lax.broadcasted_iota(jnp.int32, (rows, width), 0)


def halves(rows):
    lane = lane_iota(rows)
    return lane < 64, (lane & 32) == 0


def roll(x, shift):
    return pltpu.roll(x, shift, 1)


def split(x):
    high = x.astype(BF16)
    low = (x - high.astype(F32)).astype(BF16)
    return high, low


def dot(a, b):
    return lax.dot_general(a, b, (((1,), (0,)), ((), ())), preferred_element_type=F32)


def dot_nt(a, b):
    return lax.dot_general(a, b, (((1,), (1,)), ((), ())), preferred_element_type=F32)


def product(left, right):
    high, low = split(right)
    rows = left.shape[0] // 2
    width = right.shape[1]
    wide = dot(left, jnp.concatenate([high, low], axis=1))
    return wide[:rows, :width] + (wide[rows:, :width] + wide[:rows, width:])


def stack_split(x):
    high, low = split(x)
    return jnp.concatenate([high.astype(F32), low.astype(F32)], axis=0).astype(BF16)


def spread(columns):
    first, even = halves(8)
    tiles = []
    for column in columns[:2]:
        turned = roll(column, 64)
        for pair in (jnp.where(first, column, turned), jnp.where(first, turned, column)):
            moved = roll(pair, 32)
            tiles.append(jnp.where(even, pair, moved))
            tiles.append(jnp.where(even, moved, pair))
    pair = jnp.where(first, columns[2], roll(columns[2], 64))
    tiles.append(jnp.where(even, pair, roll(pair, 32)))
    return tiles


def group_swap(parts):
    first, even = halves(8)
    a0, a1, a2, a3 = parts
    out = []
    p = [jnp.where(first, a0, roll(a2, 64)), jnp.where(first, a1, roll(a3, 64))]
    r = [jnp.where(first, roll(a0, 64), a2), jnp.where(first, roll(a1, 64), a3)]
    for x, y in (p, r):
        out.append(jnp.where(even, x, roll(y, 32)))
        out.append(jnp.where(even, roll(x, 96), y))
    return out


def group_place(parts):
    if len(parts) < 4:
        parts = parts + [jnp.zeros((parts[0].shape[0], E * (4 - len(parts))), parts[0].dtype)]
    return jnp.concatenate(parts, axis=1)


def weigh(rows_of, x_ref, y_ref, count):
    for tile in range(M // 8):
        spans = spread([x_ref[tile * 8 : tile * 8 + 8, c * 128 : c * 128 + 128] for c in range(3)])
        for d in range(count):
            for c in range(3):
                total = rows_of[d * 16 : d * 16 + 1, c * 128 : c * 128 + 128] * spans[0]
                for p in range(1, Q):
                    total = total + rows_of[d * 16 + p : d * 16 + p + 1, c * 128 : c * 128 + 128] * spans[p]
                start = d * M + tile * 8
                y_ref[start : start + 8, c * 128 : c * 128 + 128] = total


def predict(star, left, x_ref, y_ref, first_ref, second_ref):
    y_ref[3 * M : 3 * M + 8, :] = jnp.zeros((8, W), F32)
    state = x_ref[...]
    first_ref[...] = EARLY[0] * state
    if second_ref is not None:
        second_ref[...] = LATE[0] * state

    def step(k, carry):
        weigh(star, x_ref, y_ref, 3)
        result = product(left[...], y_ref[0 : 3 * M + 8, :])
        x_ref[...] = result
        early = jnp.float32(EARLY[1])
        late = jnp.float32(LATE[1])
        for degree in range(2, TERMS):
            early = jnp.where(k == degree, EARLY[degree], early)
            late = jnp.where(k == degree, LATE[degree], late)
        first_ref[...] = first_ref[...] + early * result
        if second_ref is not None:
            second_ref[...] = second_ref[...] + late * result
        return carry

    lax.fori_loop(1, TERMS, step, 0)


def make_table(project, x, tab_ref):
    faced = product(project, x)
    for tile in range(3):
        for c in range(3):
            parts = [
                faced[f * JP + tile * 8 : f * JP + tile * 8 + 8, c * 128 : c * 128 + 128] for f in range(4)
            ]
            swapped = group_swap(parts)
            for g in range(4 if c < 2 else 1):
                row = (c * 4 + g) * JP + tile * 8
                tab_ref[row : row + 8, :] = swapped[g]
    tab_ref[Q * JP : TAB, :] = jnp.zeros((TAB - Q * JP, LANES), F32)


def send_rows(pick, tab_ref):
    high, low = split(tab_ref[...])
    return dot_nt(pick, high) + dot_nt(pick, low)


def off_rank():
    return lax.axis_index("off")


def turned_around():
    return 16 - 16 * lax.rem(lax.axis_index("fault"), 2)


def put_sends(rows, far_ref, chip_ref, self_ref, off_refs):
    chip_ref[...] = rows[0:16]
    far_ref[...] = rows[16:32]
    self_ref[...] = rows[32:48]
    for k, ref in enumerate(off_refs):
        ref[...] = rows[48 + 16 * k : 64 + 16 * k]


def first_kernel(n_off, *refs):
    sources = refs[:10]
    landed = refs[-7:-1] + refs[10:14]
    copies = [
        pltpu.make_async_copy(source, target, refs[-1].at[k])
        for k, (source, target) in enumerate(zip(sources, landed))
    ]
    for copy in copies:
        copy.start()
    state_in, star_in, stiff_in, proj_in, elem_in, face_in = landed[:6]
    refs = refs[14:-7]
    (state_out, first_out, second_out, star_out, left_out, proj_out, tab_out, pick_out, far, chip, own) = refs[:11]
    offs = refs[11 : 11 + n_off - 1]
    x_ref, y_ref, tall, slot_pad = refs[11 + n_off - 1 :]
    tall[...] = jnp.zeros((W, LANES), F32)
    slot_pad[...] = jnp.zeros((8, LANES), jnp.int32)
    for copy in copies:
        copy.wait()
    for q in range(Q):
        tall[q * E : q * E + E, 0:M] = state_in[q]
    state = tall[...].T[0:M, :]
    x_ref[...] = state
    state_out[...] = state
    for d in range(3):
        for c in range(3):
            star_out[d * 16 : d * 16 + Q, c * 128 : c * 128 + 128] = group_place(
                [star_in[q, :, d, :] for q in range(4 * c, min(4 * c + 4, Q))]
            )
    tall[...] = jnp.zeros((W, LANES), F32)
    for d in range(3):
        tall[d * M : d * M + M, 0:M] = stiff_in[d]
    left_out[...] = stack_split(tall[0:256, :].T[0:M, 0 : 3 * M + 8])
    tall[0 : 4 * JP, :] = jnp.zeros((4 * JP, LANES), F32)
    for f in range(4):
        tall[f * JP : f * JP + J, 0:M] = proj_in[:, f, :]
    proj_out[...] = stack_split(tall[0 : 4 * JP, 0:M])
    slots = elem_in.shape[2]
    slot_pad[0:1, 0:slots] = face_in[0] * E + elem_in[0] + 1
    rows = 32 + 16 * n_off
    row = row_iota(rows)
    block = row >> 4
    within = row & 15
    target = lax.rem(block - 2 + off_rank(), n_off)
    slot = jnp.where(row < 32, row ^ turned_around(), jnp.where(within < SO, 32 + target * SO + within, -1))
    wanted = jnp.where(lane_iota(rows) == slot, slot_pad[0:1, :], 0)
    entry = jnp.sum(wanted.astype(F32), axis=1, keepdims=True)
    pick = jnp.where(lane_iota(rows).astype(F32) + 1.0 == entry, 1.0, 0.0).astype(BF16)
    pick_out[...] = pick

    predict(star_out, left_out, x_ref, y_ref, first_out, second_out)
    make_table(proj_out[...], first_out[...], tab_out)
    put_sends(send_rows(pick, tab_out), far, chip, own, offs)


def gather_local(pick, tab_ref):
    high, low = split(tab_ref[0 : Q * JP + 8, :])
    return dot(high, pick) + dot(low, pick)


def side_kernel(
    n_off,
    first_in,
    star,
    tab,
    local_in,
    nbr_in,
    vol_in,
    minus_in,
    turn_in,
    lift_in,
    index_in,
    orient_in,
    cluster_in,
    source_elem,
    source_in,
    part_out,
    coef_out,
    fnbr_out,
    left_out,
    lift_out,
    here_out,
    pick_here_out,
    pick_far_out,
    flags_out,
    source_out,
    y_ref,
    tall,
    turn_pad,
    lift_pad,
    ipad,
):
    coef_out[0:48, :] = star[...]
    for f in range(4):
        for c in range(3):
            coef_out[(3 + f) * 16 : (3 + f) * 16 + Q, c * 128 : c * 128 + 128] = group_place(
                [local_in[q, :, f, :] for q in range(4 * c, min(4 * c + 4, Q))]
            )
    for q in range(Q):
        fnbr_out[q * 16 : q * 16 + Q, :] = group_place([nbr_in[q, :, f, :] for f in range(4)])
    tall[...] = jnp.zeros((512, LANES), F32)
    for d in range(3):
        tall[d * M : d * M + M, 0:M] = vol_in[d]
    for f in range(4):
        tall[(3 + f) * M : (4 + f) * M, 0:M] = minus_in[f]
    left_out[...] = stack_split(tall[...].T[0:M, 0 : 7 * M + 8])
    turn_pad[...] = jnp.zeros((3 * JP, LANES), F32)
    for o in range(3):
        turn_pad[o * JP : o * JP + J, 0:J] = turn_in[o]
    tall[...] = jnp.zeros((512, LANES), F32)
    lift_pad[...] = jnp.zeros((LANES, LANES), F32)
    for f in range(4):
        lift_pad[0:J, 0:M] = lift_in[:, f, :]
        tall[f * 3 * JP : (f + 1) * 3 * JP, :] = lax.dot_general(
            turn_pad[...],
            lift_pad[...],
            (((1,), (0,)), ((), ())),
            precision=lax.Precision.HIGHEST,
            preferred_element_type=F32,
        )
    lift_out[...] = stack_split(tall[...].T[0:M, 0 : 12 * JP])
    ipad[...] = jnp.zeros((8, LANES), jnp.int32)
    index_row = group_place([index_in[f : f + 1, :] for f in range(4)])
    ipad[0:4, 0:E] = orient_in[...]
    ipad[4:5, 0:E] = cluster_in[...]
    orient = ipad[...]
    twice = orient + roll(orient, 64)
    flags_out[...] = twice + roll(twice, 32)
    pick_here = jnp.where(row_iota(LANES) == index_row, 1.0, 0.0).astype(BF16)
    pick_here_out[...] = pick_here
    rows = 32 + 16 * n_off
    row = row_iota(rows)
    within = row & 15
    source = lax.rem(off_rank() + n_off + 2 - (row >> 4), n_off)
    place = jnp.where(
        row < 32, LANES + (row ^ turned_around()), jnp.where(within < SO, LANES + 32 + source * SO + within, -1)
    )
    pick_far_out[...] = jnp.where(place == index_row, 1.0, 0.0).astype(BF16)
    here_out[...] = gather_local(pick_here, tab)
    tall[...] = jnp.zeros((512, LANES), F32)
    for q in range(Q):
        tall[q * SRC : q * SRC + SRC, 0:M] = source_in[q]
    origin = (lax.axis_index("fault") * n_off + off_rank()) * E
    row = row_iota(SRC)
    ipad[0:1, 0:SRC] = source_elem[...] - origin
    lane = lane_iota(SRC)
    here = jnp.where(lane == row, ipad[0:1, :], 0).astype(F32)
    goal = jnp.sum(here, axis=1, keepdims=True).astype(jnp.int32)
    y_ref[0 : Q * SRC, :] = jnp.zeros((Q * SRC, W), F32)
    for q in range(Q):
        lane_in = lane - 32 * (q % 4)
        hit = jnp.logical_and(lane_in == goal, jnp.logical_and(goal >= 0, goal < E))
        c = q // 4
        y_ref[q * SRC : q * SRC + SRC, c * 128 : c * 128 + 128] = jnp.where(hit, 1.0, 0.0)
    picks = y_ref[0 : Q * SRC, :].astype(BF16)
    terms = tall[0:256, :].T[0:M, 0 : Q * SRC]
    high, low = split(terms)
    rest = (terms - high.astype(F32) - low.astype(F32)).astype(BF16)
    source_out[...] = dot(high, picks) + (dot(low, picks) + dot(rest, picks))

    weigh(coef_out, first_in, y_ref, 7)
    y_ref[7 * M : 7 * M + 8, :] = jnp.zeros((8, W), F32)
    part_out[...] = product(left_out[...], y_ref[...])


def arrive(chip, far, own, offs, pick_far, stage):
    stage[0:16, :] = chip[...]
    stage[16:32, :] = far[...]
    stage[32:48, :] = own[...]
    for k, ref in enumerate(offs):
        stage[48 + 16 * k : 64 + 16 * k, :] = ref[...]
    turned = stage[...].T[0 : Q * JP + 8, :]
    high, low = split(turned)
    return dot(high, pick_far[...]) + dot(low, pick_far[...])


def neighbour_flux(near_ref, fnbr, flags, lift, y_ref):
    for tile in range(3):
        near = [near_ref[p * JP + tile * 8 : p * JP + tile * 8 + 8, :] for p in range(Q)]
        fluxes = []
        for q in range(Q):
            total = fnbr[q * 16 : q * 16 + 1, :] * near[0]
            for p in range(1, Q):
                total = total + fnbr[q * 16 + p : q * 16 + p + 1, :] * near[p]
            fluxes.append(total)
        zero = jnp.zeros((8, LANES), F32)
        for c in range(3):
            parts = [fluxes[4 * c + g] if 4 * c + g < Q else zero for g in range(4)]
            swapped = group_swap(parts)
            for f in range(4):
                facing = flags[f : f + 1, :]
                for o in range(3):
                    start = (f * 3 + o) * JP + tile * 8
                    y_ref[start : start + 8, c * 128 : c * 128 + 128] = jnp.where(
                        facing == o, swapped[f], 0.0
                    )
    return product(lift[...], y_ref[0 : 12 * JP, :])


def wide_fine(flags):
    row = flags[4:5, :] == 1
    return row


def middle_kernel(
    n_off, state, second, part, here, fnbr, flags, lift, star, left, proj, pick, pick_far, own, chip, far, *refs
):
    offs = refs[: n_off - 1]
    outs = refs[n_off - 1 :]
    near_out, half_out, later_out, tab_out, far_out, chip_out, own_out = outs[:7]
    off_outs = outs[7 : 7 + n_off - 1]
    x_ref, y_ref, stage, acc = outs[7 + n_off - 1 :]
    near_out[...] = here[...] + arrive(chip, far, own, offs, pick_far, stage)
    total = part[...] + neighbour_flux(near_out, fnbr, flags, lift, y_ref)
    fine = jnp.concatenate([wide_fine(flags)] * 3, axis=1)
    base = state[...]
    half = jnp.where(fine, base + total, base)
    half_out[...] = half
    x_ref[...] = half
    predict(star, left, x_ref, y_ref, acc, None)
    later = jnp.where(fine, acc[...], second[...])
    later_out[...] = later
    make_table(proj[...], later, tab_out)
    put_sends(send_rows(pick[...], tab_out), far_out, chip_out, own_out, off_outs)


def late_side_kernel(
    first, second, later, half, source, near_first, tab, coef, left, flags, pick_here, base_out, here_out, x_ref, y_ref
):
    row = wide_fine(flags)
    fine = jnp.concatenate([row] * 3, axis=1)
    x_ref[...] = jnp.where(fine, later[...], first[...] + second[...])
    weigh(coef, x_ref, y_ref, 7)
    y_ref[7 * M : 7 * M + 8, :] = jnp.zeros((8, W), F32)
    base_out[...] = half[...] + source[...] + product(left[...], y_ref[...])
    here_out[...] = gather_local(pick_here[...], tab) + jnp.where(row, 0.0, near_first[...])


def last_kernel(n_off, base, here, fnbr, flags, lift, pick_far, own, chip, far, *refs):
    offs = refs[: n_off - 1]
    out, near, y_ref, stage, tall = refs[n_off - 1 :]
    tall[M:LANES, :] = jnp.zeros((LANES - M, W), F32)
    near[...] = here[...] + arrive(chip, far, own, offs, pick_far, stage)
    total = base[...] + neighbour_flux(near, fnbr, flags, lift, y_ref)
    tall[0:M, :] = total
    turned = tall[...].T
    for q in range(Q):
        out[q] = turned[q * E : q * E + E, 0:M]


def shape(*dims, dtype=F32):
    return jax.ShapeDtypeStruct(dims, dtype)


def call(kernel, ins, outs, scratch, smem=(), hbm=(), cost=2000000):
    specs = [
        pl.BlockSpec(
            memory_space=pltpu.SMEM if k in smem else pltpu.HBM if k in hbm else pltpu.VMEM
        )
        for k in range(len(ins))
    ]
    return pl.pallas_call(
        kernel,
        in_specs=specs,
        out_specs=[pl.BlockSpec(memory_space=pltpu.VMEM)] * len(outs),
        out_shape=outs,
        scratch_shapes=scratch,
        compiler_params=pltpu.CompilerParams(vmem_limit_bytes=16 * 1024 * 1024),
        cost_estimate=pl.CostEstimate(flops=cost * 1000, bytes_accessed=cost, transcendentals=0),
    )(*ins)


def trade(far, chip, offs, n_fault, n_off):
    def exchange(offset):
        firsts = range(offset, n_fault, 2)
        pairs = [(i, (i + 1) % n_fault) for i in firsts]
        return pairs + [(j, i) for i, j in pairs]

    got = []
    got_far = lax.ppermute(far, "fault", exchange(1))
    got_chip = lax.ppermute(chip, "fault", exchange(0))
    for k, rows in enumerate(offs, 1):
        got.append(lax.ppermute(rows, "off", [(j, (j + k) % n_off) for j in range(n_off)]))
    return got_chip, got_far, got


def on_device(
    n_fault,
    n_off,
    modal_state,
    star_mats,
    flux_local,
    flux_nbr,
    stiff_time,
    stiff_vol,
    flux_minus,
    face_proj,
    face_turn,
    face_lift,
    cluster,
    send_elem,
    send_face,
    nbr_index,
    orientation,
    source_elem,
    source_term,
):
    vmem = pltpu.VMEM
    rows = 32 + 16 * n_off
    wide = shape(M, W)
    table = shape(TAB, LANES)
    block = shape(16, TAB)
    near = shape(Q * JP + 8, LANES)
    given = (
        jnp.transpose(modal_state, (0, 2, 1)),
        jnp.transpose(star_mats, (1, 2, 0, 3)),
        stiff_time,
        jnp.transpose(face_proj, (2, 0, 1)),
        send_elem,
        send_face,
        nbr_index,
        orientation,
        cluster.reshape(1, E),
        source_elem.reshape(1, SRC),
    )
    outs = call(
        functools.partial(first_kernel, n_off),
        [pltpu.with_memory_space_constraint(x, pltpu.HBM) for x in given],
        [shape(*x.shape, dtype=x.dtype) for x in given[6:]]
        + [
            wide,
            wide,
            wide,
            shape(48, W),
            shape(2 * M, 3 * M + 8, dtype=BF16),
            shape(8 * JP, M, dtype=BF16),
            table,
            shape(rows, LANES, dtype=BF16),
        ]
        + [block] * (3 + n_off - 1),
        [
            vmem((M, W), F32),
            vmem((3 * M + 8, W), F32),
            vmem((W, LANES), F32),
            vmem((8, LANES), jnp.int32),
        ]
        + [vmem(x.shape, x.dtype) for x in given[:6]]
        + [pltpu.SemaphoreType.DMA((len(given),))],
        hbm=range(len(given)),
    )
    index, orient, fine, spots = outs[:4]
    outs = outs[4:]
    state, first, second, star, left, proj, tab, pick, far, chip, own = outs[:11]
    got_chip, got_far, got_off = trade(far, chip, outs[11:], n_fault, n_off)
    part, coef, fnbr, left_all, lift, here, pick_here, pick_far, flags, source = call(
        functools.partial(side_kernel, n_off),
        (
            first,
            star,
            tab,
            jnp.transpose(flux_local, (1, 2, 0, 3)),
            jnp.transpose(flux_nbr, (1, 2, 0, 3)),
            stiff_vol,
            flux_minus,
            face_turn,
            jnp.transpose(face_lift, (1, 0, 2)),
            index,
            orient,
            fine,
            spots,
            jnp.transpose(source_term, (1, 0, 2)),
        ),
        [
            wide,
            shape(7 * 16, W),
            shape(Q * 16, LANES),
            shape(2 * M, 7 * M + 8, dtype=BF16),
            shape(2 * M, 12 * JP, dtype=BF16),
            near,
            shape(LANES, LANES, dtype=BF16),
            shape(rows, LANES, dtype=BF16),
            shape(8, LANES, dtype=jnp.int32),
            wide,
        ],
        [
            vmem((7 * M + 8, W), F32),
            vmem((512, LANES), F32),
            vmem((3 * JP, LANES), F32),
            vmem((LANES, LANES), F32),
            vmem((8, LANES), jnp.int32),
        ],
    )
    outs = call(
        functools.partial(middle_kernel, n_off),
        (state, second, part, here, fnbr, flags, lift, star, left, proj, pick, pick_far, own, got_chip, got_far, *got_off),
        [near, wide, wide, table] + [block] * (3 + n_off - 1),
        [vmem((M, W), F32), vmem((12 * JP, W), F32), vmem((rows, TAB), F32), vmem((M, W), F32)],
    )
    near_first, half, later, tab, far, chip, own = outs[:7]
    got_chip, got_far, got_off = trade(far, chip, outs[7:], n_fault, n_off)
    base, here = call(
        late_side_kernel,
        (first, second, later, half, source, near_first, tab, coef, left_all, flags, pick_here),
        [wide, near],
        [vmem((M, W), F32), vmem((7 * M + 8, W), F32)],
    )
    (result,) = call(
        functools.partial(last_kernel, n_off),
        (base, here, fnbr, flags, lift, pick_far, own, got_chip, got_far, *got_off),
        [shape(Q, E, M)],
        [vmem((Q * JP + 8, LANES), F32), vmem((12 * JP, W), F32), vmem((rows, TAB), F32), vmem((LANES, W), F32)],
    )
    return jnp.transpose(result, (0, 2, 1))


def solution(mesh):
    n_fault, n_off = mesh.shape["fault"], mesh.shape["off"]
    both = ("fault", "off")
    in_specs = (
        P(None, None, both),
        P(None, None, None, both),
        P(None, None, None, both),
        P(None, None, None, both),
        P(),
        P(),
        P(),
        P(),
        P(),
        P(),
        P(both),
        P("fault", "off", None),
        P("fault", "off", None),
        P(None, both),
        P(None, both),
        P(),
        P(),
    )
    return jax.shard_map(
        functools.partial(on_device, n_fault, n_off),
        mesh=mesh,
        in_specs=in_specs,
        out_specs=P(None, None, both),
        check_vma=False,
    )
```

```python
import functools
import math

import jax
import jax.numpy as jnp
from jax import lax
from jax.experimental import pallas as pl
from jax.experimental.pallas import tpu as pltpu
from jax.sharding import PartitionSpec as P


Q = 9
M = 56
J = 21
JP = 24
E = 32
LANES = 128
W = 384
SO = 10
SRC = 16
TERMS = 6
EARLY = [0.5 ** (k + 1) / math.factorial(k + 1) for k in range(TERMS)]
LATE = [(1.0 - 0.5 ** (k + 1)) / math.factorial(k + 1) for k in range(TERMS)]
F32 = jnp.float32
BF16 = jnp.bfloat16
TAB = 256


def lane_iota(rows, width=LANES):
    return lax.broadcasted_iota(jnp.int32, (rows, width), 1)


def row_iota(rows, width=LANES):
    return lax.broadcasted_iota(jnp.int32, (rows, width), 0)


def halves(rows):
    lane = lane_iota(rows)
    return lane < 64, (lane & 32) == 0


def roll(x, shift):
    return pltpu.roll(x, shift, 1)


def split(x):
    high = x.astype(BF16)
    low = (x - high.astype(F32)).astype(BF16)
    return high, low


def dot(a, b):
    return lax.dot_general(a, b, (((1,), (0,)), ((), ())), preferred_element_type=F32)


def dot_nt(a, b):
    return lax.dot_general(a, b, (((1,), (1,)), ((), ())), preferred_element_type=F32)


def product(left, right):
    high, low = split(right)
    rows = left.shape[0] // 2
    width = right.shape[1]
    wide = dot(left, jnp.concatenate([high, low], axis=1))
    return wide[:rows, :width] + (wide[rows:, :width] + wide[:rows, width:])


def stack_split(x):
    high, low = split(x)
    return jnp.concatenate([high.astype(F32), low.astype(F32)], axis=0).astype(BF16)


def spread(columns):
    first, even = halves(8)
    tiles = []
    for column in columns[:2]:
        turned = roll(column, 64)
        for pair in (jnp.where(first, column, turned), jnp.where(first, turned, column)):
            moved = roll(pair, 32)
            tiles.append(jnp.where(even, pair, moved))
            tiles.append(jnp.where(even, moved, pair))
    pair = jnp.where(first, columns[2], roll(columns[2], 64))
    tiles.append(jnp.where(even, pair, roll(pair, 32)))
    return tiles


def group_swap(parts):
    first, even = halves(8)
    a0, a1, a2, a3 = parts
    out = []
    p = [jnp.where(first, a0, roll(a2, 64)), jnp.where(first, a1, roll(a3, 64))]
    r = [jnp.where(first, roll(a0, 64), a2), jnp.where(first, roll(a1, 64), a3)]
    for x, y in (p, r):
        out.append(jnp.where(even, x, roll(y, 32)))
        out.append(jnp.where(even, roll(x, 96), y))
    return out


def place_rows(source, target, start, members):
    for d in members:
        for c in range(2):
            target[start + d * 16 : start + d * 16 + Q, c * 128 : c * 128 + 128] = group_place(
                [source[q, :, d, :] for q in range(4 * c, 4 * c + 4)]
            )
    target[start : start + Q, 256:W] = group_place([source[Q - 1, :, d, :] for d in members])


def group_place(parts):
    if len(parts) < 4:
        parts = parts + [jnp.zeros((parts[0].shape[0], E * (4 - len(parts))), parts[0].dtype)]
    return jnp.concatenate(parts, axis=1)


def weigh(rows_of, x_ref, y_ref, count):
    for tile in range(M // 8):
        spans = spread([x_ref[tile * 8 : tile * 8 + 8, c * 128 : c * 128 + 128] for c in range(3)])

        def mixed(row, column):
            total = rows_of[row : row + 1, column : column + 128] * spans[0]
            for p in range(1, Q):
                total = total + rows_of[row + p : row + p + 1, column : column + 128] * spans[p]
            return total

        for d in range(count):
            start = d * M + tile * 8
            for c in range(2):
                y_ref[start : start + 8, c * 128 : c * 128 + 128] = mixed(d * 16, c * 128)
        for pack in range(0, count, 4):
            total = mixed(pack * 16, 256)
            for d in range(pack, min(pack + 4, count)):
                start = d * M + tile * 8
                moved = roll(total, 128 - 32 * (d - pack)) if d > pack else total
                y_ref[start : start + 8, 256:W] = moved


def predict(star, left, x_ref, y_ref, first_ref, second_ref):
    y_ref[3 * M : 3 * M + 8, :] = jnp.zeros((8, W), F32)
    state = x_ref[...]
    first_ref[...] = EARLY[0] * state
    if second_ref is not None:
        second_ref[...] = LATE[0] * state
    for k in range(1, TERMS):
        weigh(star, x_ref, y_ref, 3)
        result = product(left[...], y_ref[0 : 3 * M + 8, :])
        x_ref[...] = result
        first_ref[...] = first_ref[...] + EARLY[k] * result
        if second_ref is not None:
            second_ref[...] = second_ref[...] + LATE[k] * result


def make_table(project, x, tab_ref):
    high = x.astype(BF16).astype(F32)
    faced = dot(project, jnp.concatenate([high, high, x - high], axis=0).astype(BF16))
    for tile in range(3):
        for c in range(3):
            parts = [
                faced[f * JP + tile * 8 : f * JP + tile * 8 + 8, c * 128 : c * 128 + 128] for f in range(4)
            ]
            swapped = group_swap(parts)
            for g in range(4 if c < 2 else 1):
                row = (c * 4 + g) * JP + tile * 8
                tab_ref[row : row + 8, :] = swapped[g]
    tab_ref[Q * JP : TAB, :] = jnp.zeros((TAB - Q * JP, LANES), F32)


def send_rows(pick, tab_ref):
    high, low = split(tab_ref[...])
    return dot_nt(pick, high) + dot_nt(pick, low)


def off_rank():
    return lax.axis_index("off")


def turned_around():
    return 16 - 16 * lax.rem(lax.axis_index("fault"), 2)


def put_sends(rows, far_ref, chip_ref, self_ref, off_refs):
    chip_ref[...] = rows[0:16]
    far_ref[...] = rows[16:32]
    self_ref[...] = rows[32:48]
    for k, ref in enumerate(off_refs):
        ref[...] = rows[48 + 16 * k : 64 + 16 * k]


def first_kernel(n_off, *refs):
    sources = refs[:10]
    landed = refs[-7:-1] + refs[10:14]
    copies = [
        pltpu.make_async_copy(source, target, refs[-1].at[k])
        for k, (source, target) in enumerate(zip(sources, landed))
    ]
    for copy in copies:
        copy.start()
    state_in, star_in, stiff_in, proj_in, elem_in, face_in = landed[:6]
    refs = refs[14:-7]
    (state_out, first_out, second_out, star_out, left_out, proj_out, tab_out, pick_out, far, chip, own) = refs[:11]
    offs = refs[11 : 11 + n_off - 1]
    x_ref, y_ref, tall, slot_pad = refs[11 + n_off - 1 :]
    tall[...] = jnp.zeros((W, LANES), F32)
    slot_pad[...] = jnp.zeros((8, LANES), jnp.int32)
    for copy in copies:
        copy.wait()
    for q in range(Q):
        tall[q * E : q * E + E, 0:M] = state_in[q]
    state = tall[...].T[0:M, :]
    x_ref[...] = state
    state_out[...] = state
    star_out[...] = jnp.zeros((48, W), F32)
    place_rows(star_in, star_out, 0, range(3))
    tall[...] = jnp.zeros((W, LANES), F32)
    for d in range(3):
        tall[d * M : d * M + M, 0:M] = stiff_in[d]
    left_out[...] = stack_split(tall[0:256, :].T[0:M, 0 : 3 * M + 8])
    tall[0 : 4 * JP, :] = jnp.zeros((4 * JP, LANES), F32)
    for f in range(4):
        tall[f * JP : f * JP + J, 0:M] = proj_in[:, f, :]
    values = tall[0 : 4 * JP, :].T[0:M]
    high = values.astype(BF16).astype(F32)
    stacked = jnp.concatenate([high, values - high, high, jnp.zeros((LANES * 2 - 3 * M, 4 * JP), F32)], axis=0)
    proj_out[...] = stacked.T[:, 0 : 3 * M].astype(BF16)
    slots = elem_in.shape[2]
    slot_pad[0:1, 0:slots] = face_in[0] * E + elem_in[0] + 1
    rows = 32 + 16 * n_off
    row = row_iota(rows)
    block = row >> 4
    within = row & 15
    target = lax.rem(block - 2 + off_rank(), n_off)
    slot = jnp.where(row < 32, row ^ turned_around(), jnp.where(within < SO, 32 + target * SO + within, -1))
    wanted = jnp.where(lane_iota(rows) == slot, slot_pad[0:1, :], 0)
    entry = jnp.sum(wanted.astype(F32), axis=1, keepdims=True)
    pick = jnp.where(lane_iota(rows).astype(F32) + 1.0 == entry, 1.0, 0.0).astype(BF16)
    pick_out[...] = pick

    predict(star_out, left_out, x_ref, y_ref, first_out, second_out)
    make_table(proj_out[...], first_out[...], tab_out)
    put_sends(send_rows(pick, tab_out), far, chip, own, offs)


def gather_local(pick, tab_ref):
    high, low = split(tab_ref[0 : Q * JP + 8, :])
    return dot(high, pick) + dot(low, pick)


def side_kernel(
    n_off,
    first_in,
    star,
    tab,
    local_in,
    nbr_in,
    vol_in,
    minus_in,
    turn_in,
    lift_in,
    index_in,
    orient_in,
    cluster_in,
    source_elem,
    source_in,
    part_out,
    coef_out,
    fnbr_out,
    left_out,
    lift_out,
    here_out,
    pick_here_out,
    pick_far_out,
    flags_out,
    source_out,
    y_ref,
    tall,
    turn_pad,
    lift_pad,
    ipad,
):
    coef_out[...] = jnp.zeros((7 * 16, W), F32)
    place_rows(local_in, coef_out, 0, range(4))
    coef_out[4 * 16 : 7 * 16, :] = star[...]
    for q in range(Q):
        fnbr_out[q * 16 : q * 16 + Q, :] = group_place([nbr_in[q, :, f, :] for f in range(4)])
    tall[...] = jnp.zeros((512, LANES), F32)
    for f in range(4):
        tall[f * M : f * M + M, 0:M] = minus_in[f]
    for d in range(3):
        tall[(4 + d) * M : (5 + d) * M, 0:M] = vol_in[d]
    left_out[...] = stack_split(tall[...].T[0:M, 0 : 7 * M + 8])
    turn_pad[...] = jnp.zeros((3 * JP, LANES), F32)
    for o in range(3):
        turn_pad[o * JP : o * JP + J, 0:J] = turn_in[o]
    tall[...] = jnp.zeros((512, LANES), F32)
    lift_pad[...] = jnp.zeros((LANES, LANES), F32)
    for f in range(4):
        lift_pad[0:J, 0:M] = lift_in[:, f, :]
        tall[f * 3 * JP : (f + 1) * 3 * JP, :] = lax.dot_general(
            turn_pad[...],
            lift_pad[...],
            (((1,), (0,)), ((), ())),
            precision=lax.Precision.HIGHEST,
            preferred_element_type=F32,
        )
    lift_out[...] = stack_split(tall[...].T[0:M, 0 : 12 * JP])
    ipad[...] = jnp.zeros((8, LANES), jnp.int32)
    index_row = group_place([index_in[f : f + 1, :] for f in range(4)])
    ipad[0:4, 0:E] = orient_in[...]
    ipad[4:5, 0:E] = cluster_in[...]
    orient = ipad[...]
    twice = orient + roll(orient, 64)
    flags_out[...] = twice + roll(twice, 32)
    pick_here = jnp.where(row_iota(LANES) == index_row, 1.0, 0.0).astype(BF16)
    pick_here_out[...] = pick_here
    rows = 32 + 16 * n_off
    row = row_iota(rows)
    within = row & 15
    source = lax.rem(off_rank() + n_off + 2 - (row >> 4), n_off)
    place = jnp.where(
        row < 32, LANES + (row ^ turned_around()), jnp.where(within < SO, LANES + 32 + source * SO + within, -1)
    )
    pick_far_out[...] = jnp.where(place == index_row, 1.0, 0.0).astype(BF16)
    here_out[...] = gather_local(pick_here, tab)
    tall[...] = jnp.zeros((512, LANES), F32)
    for q in range(Q):
        tall[q * SRC : q * SRC + SRC, 0:M] = source_in[q]
    origin = (lax.axis_index("fault") * n_off + off_rank()) * E
    row = row_iota(SRC)
    ipad[0:1, 0:SRC] = source_elem[...] - origin
    lane = lane_iota(SRC)
    here = jnp.where(lane == row, ipad[0:1, :], 0).astype(F32)
    goal = jnp.sum(here, axis=1, keepdims=True).astype(jnp.int32)
    y_ref[0 : Q * SRC, :] = jnp.zeros((Q * SRC, W), F32)
    for q in range(Q):
        lane_in = lane - 32 * (q % 4)
        hit = jnp.logical_and(lane_in == goal, jnp.logical_and(goal >= 0, goal < E))
        c = q // 4
        y_ref[q * SRC : q * SRC + SRC, c * 128 : c * 128 + 128] = jnp.where(hit, 1.0, 0.0)
    picks = y_ref[0 : Q * SRC, :].astype(BF16)
    terms = tall[0:256, :].T[0:M, 0 : Q * SRC]
    high, low = split(terms)
    rest = (terms - high.astype(F32) - low.astype(F32)).astype(BF16)
    source_out[...] = dot(high, picks) + (dot(low, picks) + dot(rest, picks))

    weigh(coef_out, first_in, y_ref, 7)
    y_ref[7 * M : 7 * M + 8, :] = jnp.zeros((8, W), F32)
    part_out[...] = product(left_out[...], y_ref[...])


def arrive(chip, far, own, offs, pick_far, stage):
    stage[0:16, :] = chip[...]
    stage[16:32, :] = far[...]
    stage[32:48, :] = own[...]
    for k, ref in enumerate(offs):
        stage[48 + 16 * k : 64 + 16 * k, :] = ref[...]
    turned = stage[...].T[0 : Q * JP + 8, :]
    high, low = split(turned)
    return dot(high, pick_far[...]) + dot(low, pick_far[...])


def neighbour_flux(near_ref, fnbr, flags, lift, y_ref):
    for tile in range(3):
        near = [near_ref[p * JP + tile * 8 : p * JP + tile * 8 + 8, :] for p in range(Q)]
        fluxes = []
        for q in range(Q):
            total = fnbr[q * 16 : q * 16 + 1, :] * near[0]
            for p in range(1, Q):
                total = total + fnbr[q * 16 + p : q * 16 + p + 1, :] * near[p]
            fluxes.append(total)
        zero = jnp.zeros((8, LANES), F32)
        for c in range(3):
            parts = [fluxes[4 * c + g] if 4 * c + g < Q else zero for g in range(4)]
            swapped = group_swap(parts)
            for f in range(4):
                facing = flags[f : f + 1, :]
                for o in range(3):
                    start = (f * 3 + o) * JP + tile * 8
                    y_ref[start : start + 8, c * 128 : c * 128 + 128] = jnp.where(
                        facing == o, swapped[f], 0.0
                    )
    return product(lift[...], y_ref[0 : 12 * JP, :])


def wide_fine(flags):
    row = flags[4:5, :] == 1
    return row


def middle_kernel(
    n_off, state, second, part, here, fnbr, flags, lift, star, left, proj, pick, pick_far, own, chip, far, *refs
):
    offs = refs[: n_off - 1]
    outs = refs[n_off - 1 :]
    near_out, half_out, later_out, tab_out, far_out, chip_out, own_out = outs[:7]
    off_outs = outs[7 : 7 + n_off - 1]
    x_ref, y_ref, stage, acc = outs[7 + n_off - 1 :]
    near_out[...] = here[...] + arrive(chip, far, own, offs, pick_far, stage)
    total = part[...] + neighbour_flux(near_out, fnbr, flags, lift, y_ref)
    fine = jnp.concatenate([wide_fine(flags)] * 3, axis=1)
    base = state[...]
    half = jnp.where(fine, base + total, base)
    half_out[...] = half
    x_ref[...] = half
    predict(star, left, x_ref, y_ref, acc, None)
    later = jnp.where(fine, acc[...], second[...])
    later_out[...] = later
    make_table(proj[...], later, tab_out)
    put_sends(send_rows(pick[...], tab_out), far_out, chip_out, own_out, off_outs)


def late_side_kernel(
    first, second, later, half, source, near_first, tab, coef, left, flags, pick_here, base_out, here_out, x_ref, y_ref
):
    row = wide_fine(flags)
    fine = jnp.concatenate([row] * 3, axis=1)
    x_ref[...] = jnp.where(fine, later[...], first[...] + second[...])
    weigh(coef, x_ref, y_ref, 7)
    y_ref[7 * M : 7 * M + 8, :] = jnp.zeros((8, W), F32)
    base_out[...] = half[...] + source[...] + product(left[...], y_ref[...])
    here_out[...] = gather_local(pick_here[...], tab) + jnp.where(row, 0.0, near_first[...])


def last_kernel(n_off, base, here, fnbr, flags, lift, pick_far, own, chip, far, *refs):
    offs = refs[: n_off - 1]
    out, near, y_ref, stage, tall = refs[n_off - 1 :]
    tall[M:LANES, :] = jnp.zeros((LANES - M, W), F32)
    near[...] = here[...] + arrive(chip, far, own, offs, pick_far, stage)
    total = base[...] + neighbour_flux(near, fnbr, flags, lift, y_ref)
    tall[0:M, :] = total
    turned = tall[...].T
    for q in range(Q):
        out[q] = turned[q * E : q * E + E, 0:M]


def shape(*dims, dtype=F32):
    return jax.ShapeDtypeStruct(dims, dtype)


def call(kernel, ins, outs, scratch, smem=(), hbm=(), cost=2000000):
    specs = [
        pl.BlockSpec(
            memory_space=pltpu.SMEM if k in smem else pltpu.HBM if k in hbm else pltpu.VMEM
        )
        for k in range(len(ins))
    ]
    return pl.pallas_call(
        kernel,
        in_specs=specs,
        out_specs=[pl.BlockSpec(memory_space=pltpu.VMEM)] * len(outs),
        out_shape=outs,
        scratch_shapes=scratch,
        compiler_params=pltpu.CompilerParams(vmem_limit_bytes=16 * 1024 * 1024),
        cost_estimate=pl.CostEstimate(flops=cost * 1000, bytes_accessed=cost, transcendentals=0),
    )(*ins)


def trade(far, chip, offs, n_fault, n_off):
    def exchange(offset):
        firsts = range(offset, n_fault, 2)
        pairs = [(i, (i + 1) % n_fault) for i in firsts]
        return pairs + [(j, i) for i, j in pairs]

    got = []
    got_far = lax.ppermute(far, "fault", exchange(1))
    got_chip = lax.ppermute(chip, "fault", exchange(0))
    for k, rows in enumerate(offs, 1):
        got.append(lax.ppermute(rows, "off", [(j, (j + k) % n_off) for j in range(n_off)]))
    return got_chip, got_far, got


def on_device(
    n_fault,
    n_off,
    modal_state,
    star_mats,
    flux_local,
    flux_nbr,
    stiff_time,
    stiff_vol,
    flux_minus,
    face_proj,
    face_turn,
    face_lift,
    cluster,
    send_elem,
    send_face,
    nbr_index,
    orientation,
    source_elem,
    source_term,
):
    vmem = pltpu.VMEM
    rows = 32 + 16 * n_off
    wide = shape(M, W)
    table = shape(TAB, LANES)
    block = shape(16, TAB)
    near = shape(Q * JP + 8, LANES)
    given = (
        jnp.transpose(modal_state, (0, 2, 1)),
        jnp.transpose(star_mats, (1, 2, 0, 3)),
        stiff_time,
        jnp.transpose(face_proj, (2, 0, 1)),
        send_elem,
        send_face,
        nbr_index,
        orientation,
        cluster.reshape(1, E),
        source_elem.reshape(1, SRC),
    )
    outs = call(
        functools.partial(first_kernel, n_off),
        [pltpu.with_memory_space_constraint(x, pltpu.HBM) for x in given],
        [shape(*x.shape, dtype=x.dtype) for x in given[6:]]
        + [
            wide,
            wide,
            wide,
            shape(48, W),
            shape(2 * M, 3 * M + 8, dtype=BF16),
            shape(4 * JP, 3 * M, dtype=BF16),
            table,
            shape(rows, LANES, dtype=BF16),
        ]
        + [block] * (3 + n_off - 1),
        [
            vmem((M, W), F32),
            vmem((3 * M + 8, W), F32),
            vmem((W, LANES), F32),
            vmem((8, LANES), jnp.int32),
        ]
        + [vmem(x.shape, x.dtype) for x in given[:6]]
        + [pltpu.SemaphoreType.DMA((len(given),))],
        hbm=range(len(given)),
    )
    index, orient, fine, spots = outs[:4]
    outs = outs[4:]
    state, first, second, star, left, proj, tab, pick, far, chip, own = outs[:11]
    got_chip, got_far, got_off = trade(far, chip, outs[11:], n_fault, n_off)
    part, coef, fnbr, left_all, lift, here, pick_here, pick_far, flags, source = call(
        functools.partial(side_kernel, n_off),
        (
            first,
            star,
            tab,
            jnp.transpose(flux_local, (1, 2, 0, 3)),
            jnp.transpose(flux_nbr, (1, 2, 0, 3)),
            stiff_vol,
            flux_minus,
            face_turn,
            jnp.transpose(face_lift, (1, 0, 2)),
            index,
            orient,
            fine,
            spots,
            jnp.transpose(source_term, (1, 0, 2)),
        ),
        [
            wide,
            shape(7 * 16, W),
            shape(Q * 16, LANES),
            shape(2 * M, 7 * M + 8, dtype=BF16),
            shape(2 * M, 12 * JP, dtype=BF16),
            near,
            shape(LANES, LANES, dtype=BF16),
            shape(rows, LANES, dtype=BF16),
            shape(8, LANES, dtype=jnp.int32),
            wide,
        ],
        [
            vmem((7 * M + 8, W), F32),
            vmem((512, LANES), F32),
            vmem((3 * JP, LANES), F32),
            vmem((LANES, LANES), F32),
            vmem((8, LANES), jnp.int32),
        ],
    )
    outs = call(
        functools.partial(middle_kernel, n_off),
        (state, second, part, here, fnbr, flags, lift, star, left, proj, pick, pick_far, own, got_chip, got_far, *got_off),
        [near, wide, wide, table] + [block] * (3 + n_off - 1),
        [vmem((M, W), F32), vmem((12 * JP, W), F32), vmem((rows, TAB), F32), vmem((M, W), F32)],
    )
    near_first, half, later, tab, far, chip, own = outs[:7]
    got_chip, got_far, got_off = trade(far, chip, outs[7:], n_fault, n_off)
    base, here = call(
        late_side_kernel,
        (first, second, later, half, source, near_first, tab, coef, left_all, flags, pick_here),
        [wide, near],
        [vmem((M, W), F32), vmem((7 * M + 8, W), F32)],
    )
    (result,) = call(
        functools.partial(last_kernel, n_off),
        (base, here, fnbr, flags, lift, pick_far, own, got_chip, got_far, *got_off),
        [shape(Q, E, M)],
        [vmem((Q * JP + 8, LANES), F32), vmem((12 * JP, W), F32), vmem((rows, TAB), F32), vmem((LANES, W), F32)],
    )
    return jnp.transpose(result, (0, 2, 1))


def solution(mesh):
    n_fault, n_off = mesh.shape["fault"], mesh.shape["off"]
    both = ("fault", "off")
    in_specs = (
        P(None, None, both),
        P(None, None, None, both),
        P(None, None, None, both),
        P(None, None, None, both),
        P(),
        P(),
        P(),
        P(),
        P(),
        P(),
        P(both),
        P("fault", "off", None),
        P("fault", "off", None),
        P(None, both),
        P(None, both),
        P(),
        P(),
    )
    return jax.shard_map(
        functools.partial(on_device, n_fault, n_off),
        mesh=mesh,
        in_specs=in_specs,
        out_specs=P(None, None, both),
        check_vma=False,
    )
```

```python
import functools
import math

import jax
import jax.numpy as jnp
from jax import lax
from jax.experimental import pallas as pl
from jax.experimental.pallas import tpu as pltpu
from jax.sharding import PartitionSpec as P


Q = 9
M = 56
J = 21
JP = 24
E = 32
LANES = 128
W = 384
SO = 10
SRC = 16
TERMS = 6
EARLY = [0.5 ** (k + 1) / math.factorial(k + 1) for k in range(TERMS)]
LATE = [(1.0 - 0.5 ** (k + 1)) / math.factorial(k + 1) for k in range(TERMS)]
F32 = jnp.float32
BF16 = jnp.bfloat16
TAB = 256


def lane_iota(rows, width=LANES):
    return lax.broadcasted_iota(jnp.int32, (rows, width), 1)


def row_iota(rows, width=LANES):
    return lax.broadcasted_iota(jnp.int32, (rows, width), 0)


def halves(rows):
    lane = lane_iota(rows)
    return lane < 64, (lane & 32) == 0


def roll(x, shift):
    return pltpu.roll(x, shift, 1)


def split(x):
    high = x.astype(BF16)
    low = (x - high.astype(F32)).astype(BF16)
    return high, low


def dot(a, b):
    return lax.dot_general(a, b, (((1,), (0,)), ((), ())), preferred_element_type=F32)


def dot_nt(a, b):
    return lax.dot_general(a, b, (((1,), (1,)), ((), ())), preferred_element_type=F32)


def product(left, right):
    high, low = split(right)
    rows = left.shape[0] // 2
    width = right.shape[1]
    wide = dot(left, jnp.concatenate([high, low], axis=1))
    return wide[:rows, :width] + (wide[rows:, :width] + wide[:rows, width:])


def stack_split(x):
    high, low = split(x)
    return jnp.concatenate([high.astype(F32), low.astype(F32)], axis=0).astype(BF16)


def turns(columns):
    first, even = halves(8)
    tiles = []
    for column in columns[:2]:
        tiles += [column] + [roll(column, 128 - 32 * s) for s in range(1, 4)]
    pair = jnp.where(first, columns[2], roll(columns[2], 64))
    return tiles + [jnp.where(even, pair, roll(pair, 32))]


def group_swap(parts):
    first, even = halves(8)
    a0, a1, a2, a3 = parts
    out = []
    p = [jnp.where(first, a0, roll(a2, 64)), jnp.where(first, a1, roll(a3, 64))]
    r = [jnp.where(first, roll(a0, 64), a2), jnp.where(first, roll(a1, 64), a3)]
    for x, y in (p, r):
        out.append(jnp.where(even, x, roll(y, 32)))
        out.append(jnp.where(even, roll(x, 96), y))
    return out


def place_rows(source, target, start, members):
    def piece(q, d, group):
        order = [4 * c + (group + s) % 4 for c in range(2) for s in range(4)] + [Q - 1]
        return jnp.concatenate([source[q, p : p + 1, d, :] for p in order], axis=0)

    for d in members:
        for c in range(2):
            target[start + d * 16 : start + d * 16 + Q, c * 128 : c * 128 + 128] = group_place(
                [piece(4 * c + g, d, g) for g in range(4)]
            )
    target[start : start + Q, 256:W] = group_place([piece(Q - 1, d, g) for g, d in enumerate(members)])


def group_place(parts):
    if len(parts) < 4:
        parts = parts + [jnp.zeros((parts[0].shape[0], E * (4 - len(parts))), parts[0].dtype)]
    return jnp.concatenate(parts, axis=1)


def weigh(rows_of, x_ref, y_ref, count):
    for tile in range(M // 8):
        spans = turns([x_ref[tile * 8 : tile * 8 + 8, c * 128 : c * 128 + 128] for c in range(3)])

        def mixed(row, column):
            total = rows_of[row : row + 1, column : column + 128] * spans[0]
            for p in range(1, Q):
                total = total + rows_of[row + p : row + p + 1, column : column + 128] * spans[p]
            return total

        for d in range(count):
            start = (tile * count + d) * 8
            for c in range(2):
                y_ref[start : start + 8, c * 128 : c * 128 + 128] = mixed(d * 16, c * 128)
        for pack in range(0, count, 4):
            total = mixed(pack * 16, 256)
            for d in range(pack, min(pack + 4, count)):
                start = (tile * count + d) * 8
                moved = roll(total, 128 - 32 * (d - pack)) if d > pack else total
                y_ref[start : start + 8, 256:W] = moved


def order_rows(tall, matrices):
    for d, matrix in enumerate(matrices):
        for tile in range(M // 8):
            start = (tile * len(matrices) + d) * 8
            tall[start : start + 8, 0:M] = matrix[tile * 8 : tile * 8 + 8]


def predict(star, left, x_ref, y_ref, first_ref, second_ref):
    y_ref[3 * M : 3 * M + 8, :] = jnp.zeros((8, W), F32)
    state = x_ref[...]
    first_ref[...] = EARLY[0] * state
    if second_ref is not None:
        second_ref[...] = LATE[0] * state
    for k in range(1, TERMS):
        weigh(star, x_ref, y_ref, 3)
        result = product(left[...], y_ref[0 : 3 * M + 8, :])
        x_ref[...] = result
        first_ref[...] = first_ref[...] + EARLY[k] * result
        if second_ref is not None:
            second_ref[...] = second_ref[...] + LATE[k] * result


def make_table(project, x, tab_ref):
    high = x.astype(BF16).astype(F32)
    faced = dot(project, jnp.concatenate([high, high, x - high], axis=0).astype(BF16))
    for tile in range(3):
        for c in range(3):
            parts = [
                faced[f * JP + tile * 8 : f * JP + tile * 8 + 8, c * 128 : c * 128 + 128] for f in range(4)
            ]
            swapped = group_swap(parts)
            for g in range(4 if c < 2 else 1):
                row = (c * 4 + g) * JP + tile * 8
                tab_ref[row : row + 8, :] = swapped[g]
    tab_ref[Q * JP : TAB, :] = jnp.zeros((TAB - Q * JP, LANES), F32)


def send_rows(pick, tab_ref):
    high, low = split(tab_ref[...])
    return dot_nt(jnp.concatenate([pick, pick], axis=1), jnp.concatenate([high, low], axis=1))


def off_rank():
    return lax.axis_index("off")


def turned_around():
    return 16 - 16 * lax.rem(lax.axis_index("fault"), 2)


def put_sends(rows, far_ref, chip_ref, self_ref, off_refs):
    chip_ref[...] = rows[0:16]
    far_ref[...] = rows[16:32]
    self_ref[...] = rows[32:48]
    for k, ref in enumerate(off_refs):
        ref[...] = rows[48 + 16 * k : 64 + 16 * k]


def first_kernel(n_off, *refs):
    sources = refs[:10]
    landed = refs[-7:-1] + refs[10:14]
    copies = [
        pltpu.make_async_copy(source, target, refs[-1].at[k])
        for k, (source, target) in enumerate(zip(sources, landed))
    ]
    for copy in copies:
        copy.start()
    state_in, star_in, stiff_in, proj_in, elem_in, face_in = landed[:6]
    refs = refs[14:-7]
    (state_out, first_out, second_out, star_out, left_out, proj_out, tab_out, pick_out, far, chip, own) = refs[:11]
    offs = refs[11 : 11 + n_off - 1]
    x_ref, y_ref, tall, slot_pad = refs[11 + n_off - 1 :]
    tall[...] = jnp.zeros((W, LANES), F32)
    slot_pad[...] = jnp.zeros((8, LANES), jnp.int32)
    for copy in copies:
        copy.wait()
    for q in range(Q):
        tall[q * E : q * E + E, 0:M] = state_in[q]
    state = tall[...].T[0:M, :]
    x_ref[...] = state
    state_out[...] = state
    star_out[...] = jnp.zeros((48, W), F32)
    place_rows(star_in, star_out, 0, range(3))
    tall[...] = jnp.zeros((W, LANES), F32)
    order_rows(tall, [stiff_in[d] for d in range(3)])
    left_out[...] = stack_split(tall[0:256, :].T[0:M, 0 : 3 * M + 8])
    tall[0 : 4 * JP, :] = jnp.zeros((4 * JP, LANES), F32)
    for f in range(4):
        tall[f * JP : f * JP + J, 0:M] = proj_in[:, f, :]
    values = tall[0 : 4 * JP, 0:M]
    high = values.astype(BF16).astype(F32)
    proj_out[...] = jnp.concatenate([high, values - high, high], axis=1).astype(BF16)
    slots = elem_in.shape[2]
    slot_pad[0:1, 0:slots] = face_in[0] * E + elem_in[0] + 1
    rows = 32 + 16 * n_off
    row = row_iota(rows)
    block = row >> 4
    within = row & 15
    target = lax.rem(block - 2 + off_rank(), n_off)
    slot = jnp.where(row < 32, row ^ turned_around(), jnp.where(within < SO, 32 + target * SO + within, -1))
    wanted = jnp.where(lane_iota(rows) == slot, slot_pad[0:1, :], 0)
    entry = jnp.sum(wanted.astype(F32), axis=1, keepdims=True)
    pick = jnp.where(lane_iota(rows).astype(F32) + 1.0 == entry, 1.0, 0.0).astype(BF16)
    pick_out[...] = pick

    predict(star_out, left_out, x_ref, y_ref, first_out, second_out)
    make_table(proj_out[...], first_out[...], tab_out)
    put_sends(send_rows(pick, tab_out), far, chip, own, offs)


def gather_local(pick, tab_ref):
    high, low = split(tab_ref[0 : Q * JP + 8, :])
    return dot(jnp.concatenate([high, low], axis=1), jnp.concatenate([pick, pick], axis=0))


def side_kernel(
    n_off,
    first_in,
    star,
    tab,
    local_in,
    nbr_in,
    vol_in,
    minus_in,
    turn_in,
    lift_in,
    index_in,
    orient_in,
    cluster_in,
    source_elem,
    source_in,
    part_out,
    coef_out,
    fnbr_out,
    left_out,
    lift_out,
    here_out,
    pick_here_out,
    pick_far_out,
    flags_out,
    source_out,
    y_ref,
    tall,
    turn_pad,
    lift_pad,
    ipad,
):
    coef_out[...] = jnp.zeros((7 * 16, W), F32)
    place_rows(local_in, coef_out, 0, range(4))
    coef_out[4 * 16 : 7 * 16, :] = star[...]
    for q in range(Q):
        fnbr_out[q * 16 : q * 16 + Q, :] = group_place([nbr_in[q, :, f, :] for f in range(4)])
    tall[...] = jnp.zeros((512, LANES), F32)
    order_rows(tall, [minus_in[f] for f in range(4)] + [vol_in[d] for d in range(3)])
    left_out[...] = stack_split(tall[...].T[0:M, 0 : 7 * M + 8])
    turn_pad[...] = jnp.zeros((3 * JP, LANES), F32)
    for o in range(3):
        turn_pad[o * JP : o * JP + J, 0:J] = turn_in[o]
    tall[...] = jnp.zeros((512, LANES), F32)
    lift_pad[...] = jnp.zeros((LANES, LANES), F32)
    for f in range(4):
        lift_pad[0:J, 0:M] = lift_in[:, f, :]
        combined = lax.dot_general(
            turn_pad[...],
            lift_pad[...],
            (((1,), (0,)), ((), ())),
            precision=lax.Precision.HIGHEST,
            preferred_element_type=F32,
        )
        for o in range(3):
            for tile in range(3):
                start = (tile * 12 + f * 3 + o) * 8
                tall[start : start + 8, :] = combined[o * JP + tile * 8 : o * JP + tile * 8 + 8]
    lift_out[...] = stack_split(tall[...].T[0:M, 0 : 12 * JP])
    ipad[...] = jnp.zeros((8, LANES), jnp.int32)
    index_row = group_place([index_in[f : f + 1, :] for f in range(4)])
    ipad[0:4, 0:E] = orient_in[...]
    ipad[4:5, 0:E] = cluster_in[...]
    orient = ipad[...]
    twice = orient + roll(orient, 64)
    flags_out[...] = twice + roll(twice, 32)
    pick_here = jnp.where(row_iota(LANES) == index_row, 1.0, 0.0).astype(BF16)
    pick_here_out[...] = pick_here
    rows = 32 + 16 * n_off
    row = row_iota(rows)
    within = row & 15
    source = lax.rem(off_rank() + n_off + 2 - (row >> 4), n_off)
    place = jnp.where(
        row < 32, LANES + (row ^ turned_around()), jnp.where(within < SO, LANES + 32 + source * SO + within, -1)
    )
    pick_far = jnp.where(place == index_row, 1.0, 0.0)
    pick_far_out[...] = jnp.concatenate([pick_far, pick_far], axis=0).astype(BF16)
    here_out[...] = gather_local(pick_here, tab)
    tall[...] = jnp.zeros((512, LANES), F32)
    for q in range(Q):
        tall[q * SRC : q * SRC + SRC, 0:M] = source_in[q]
    origin = (lax.axis_index("fault") * n_off + off_rank()) * E
    row = row_iota(SRC)
    ipad[0:1, 0:SRC] = source_elem[...] - origin
    lane = lane_iota(SRC)
    here = jnp.where(lane == row, ipad[0:1, :], 0).astype(F32)
    goal = jnp.sum(here, axis=1, keepdims=True).astype(jnp.int32)
    y_ref[0 : Q * SRC, :] = jnp.zeros((Q * SRC, W), F32)
    for q in range(Q):
        lane_in = lane - 32 * (q % 4)
        hit = jnp.logical_and(lane_in == goal, jnp.logical_and(goal >= 0, goal < E))
        c = q // 4
        y_ref[q * SRC : q * SRC + SRC, c * 128 : c * 128 + 128] = jnp.where(hit, 1.0, 0.0)
    picks = y_ref[0 : Q * SRC, :].astype(BF16)
    terms = tall[0:256, :].T[0:M, 0 : Q * SRC]
    high, low = split(terms)
    rest = (terms - high.astype(F32) - low.astype(F32)).astype(BF16)
    source_out[...] = dot(high, picks) + (dot(low, picks) + dot(rest, picks))

    weigh(coef_out, first_in, y_ref, 7)
    y_ref[7 * M : 7 * M + 8, :] = jnp.zeros((8, W), F32)
    part_out[...] = product(left_out[...], y_ref[...])


def arrive(chip, far, own, offs, pick_far, stage):
    stage[0:16, :] = chip[...]
    stage[16:32, :] = far[...]
    stage[32:48, :] = own[...]
    for k, ref in enumerate(offs):
        stage[48 + 16 * k : 64 + 16 * k, :] = ref[...]
    rows = stage[...]
    high = rows.astype(BF16).astype(F32)
    turned = jnp.concatenate([high, rows - high], axis=0).T[0 : Q * JP + 8, :].astype(BF16)
    return dot(turned, pick_far[...])


def neighbour_flux(near_ref, fnbr, flags, lift, y_ref):
    for tile in range(3):
        near = [near_ref[p * JP + tile * 8 : p * JP + tile * 8 + 8, :] for p in range(Q)]
        fluxes = []
        for q in range(Q):
            total = fnbr[q * 16 : q * 16 + 1, :] * near[0]
            for p in range(1, Q):
                total = total + fnbr[q * 16 + p : q * 16 + p + 1, :] * near[p]
            fluxes.append(total)
        zero = jnp.zeros((8, LANES), F32)
        for c in range(3):
            parts = [fluxes[4 * c + g] if 4 * c + g < Q else zero for g in range(4)]
            swapped = group_swap(parts)
            for f in range(4):
                facing = flags[f : f + 1, :]
                for o in range(3):
                    start = (tile * 12 + f * 3 + o) * 8
                    y_ref[start : start + 8, c * 128 : c * 128 + 128] = jnp.where(
                        facing == o, swapped[f], 0.0
                    )
    return product(lift[...], y_ref[0 : 12 * JP, :])


def wide_fine(flags):
    row = flags[4:5, :] == 1
    return row


def middle_kernel(
    n_off, state, second, part, here, fnbr, flags, lift, star, left, proj, pick, pick_far, own, chip, far, *refs
):
    offs = refs[: n_off - 1]
    outs = refs[n_off - 1 :]
    near_out, half_out, later_out, tab_out, far_out, chip_out, own_out = outs[:7]
    off_outs = outs[7 : 7 + n_off - 1]
    x_ref, y_ref, stage, acc = outs[7 + n_off - 1 :]
    near_out[...] = here[...] + arrive(chip, far, own, offs, pick_far, stage)
    total = part[...] + neighbour_flux(near_out, fnbr, flags, lift, y_ref)
    fine = jnp.concatenate([wide_fine(flags)] * 3, axis=1)
    base = state[...]
    half = jnp.where(fine, base + total, base)
    half_out[...] = half
    x_ref[...] = half
    predict(star, left, x_ref, y_ref, acc, None)
    later = jnp.where(fine, acc[...], second[...])
    later_out[...] = later
    make_table(proj[...], later, tab_out)
    put_sends(send_rows(pick[...], tab_out), far_out, chip_out, own_out, off_outs)


def late_side_kernel(
    first, second, later, half, source, near_first, tab, coef, left, flags, pick_here, base_out, here_out, x_ref, y_ref
):
    row = wide_fine(flags)
    fine = jnp.concatenate([row] * 3, axis=1)
    x_ref[...] = jnp.where(fine, later[...], first[...] + second[...])
    weigh(coef, x_ref, y_ref, 7)
    y_ref[7 * M : 7 * M + 8, :] = jnp.zeros((8, W), F32)
    base_out[...] = half[...] + source[...] + product(left[...], y_ref[...])
    here_out[...] = gather_local(pick_here[...], tab) + jnp.where(row, 0.0, near_first[...])


def last_kernel(n_off, base, here, fnbr, flags, lift, pick_far, own, chip, far, *refs):
    offs = refs[: n_off - 1]
    out, near, y_ref, stage, tall = refs[n_off - 1 :]
    tall[M:LANES, :] = jnp.zeros((LANES - M, W), F32)
    near[...] = here[...] + arrive(chip, far, own, offs, pick_far, stage)
    total = base[...] + neighbour_flux(near, fnbr, flags, lift, y_ref)
    tall[0:M, :] = total
    turned = tall[...].T
    for q in range(Q):
        out[q] = turned[q * E : q * E + E, 0:M]


def shape(*dims, dtype=F32):
    return jax.ShapeDtypeStruct(dims, dtype)


def call(kernel, ins, outs, scratch, smem=(), hbm=(), cost=2000000):
    specs = [
        pl.BlockSpec(
            memory_space=pltpu.SMEM if k in smem else pltpu.HBM if k in hbm else pltpu.VMEM
        )
        for k in range(len(ins))
    ]
    return pl.pallas_call(
        kernel,
        in_specs=specs,
        out_specs=[pl.BlockSpec(memory_space=pltpu.VMEM)] * len(outs),
        out_shape=outs,
        scratch_shapes=scratch,
        compiler_params=pltpu.CompilerParams(vmem_limit_bytes=16 * 1024 * 1024),
        cost_estimate=pl.CostEstimate(flops=cost * 1000, bytes_accessed=cost, transcendentals=0),
    )(*ins)


def trade(far, chip, offs, n_fault, n_off):
    def exchange(offset):
        firsts = range(offset, n_fault, 2)
        pairs = [(i, (i + 1) % n_fault) for i in firsts]
        return pairs + [(j, i) for i, j in pairs]

    got = []
    got_far = lax.ppermute(far, "fault", exchange(1))
    got_chip = lax.ppermute(chip, "fault", exchange(0))
    for k, rows in enumerate(offs, 1):
        got.append(lax.ppermute(rows, "off", [(j, (j + k) % n_off) for j in range(n_off)]))
    return got_chip, got_far, got


def on_device(
    n_fault,
    n_off,
    modal_state,
    star_mats,
    flux_local,
    flux_nbr,
    stiff_time,
    stiff_vol,
    flux_minus,
    face_proj,
    face_turn,
    face_lift,
    cluster,
    send_elem,
    send_face,
    nbr_index,
    orientation,
    source_elem,
    source_term,
):
    vmem = pltpu.VMEM
    rows = 32 + 16 * n_off
    wide = shape(M, W)
    table = shape(TAB, LANES)
    block = shape(16, TAB)
    near = shape(Q * JP + 8, LANES)
    given = (
        jnp.transpose(modal_state, (0, 2, 1)),
        jnp.transpose(star_mats, (1, 2, 0, 3)),
        stiff_time,
        jnp.transpose(face_proj, (2, 0, 1)),
        send_elem,
        send_face,
        nbr_index,
        orientation,
        cluster.reshape(1, E),
        source_elem.reshape(1, SRC),
    )
    outs = call(
        functools.partial(first_kernel, n_off),
        [pltpu.with_memory_space_constraint(x, pltpu.HBM) for x in given],
        [shape(*x.shape, dtype=x.dtype) for x in given[6:]]
        + [
            wide,
            wide,
            wide,
            shape(48, W),
            shape(2 * M, 3 * M + 8, dtype=BF16),
            shape(4 * JP, 3 * M, dtype=BF16),
            table,
            shape(rows, LANES, dtype=BF16),
        ]
        + [block] * (3 + n_off - 1),
        [
            vmem((M, W), F32),
            vmem((3 * M + 8, W), F32),
            vmem((W, LANES), F32),
            vmem((8, LANES), jnp.int32),
        ]
        + [vmem(x.shape, x.dtype) for x in given[:6]]
        + [pltpu.SemaphoreType.DMA((len(given),))],
        hbm=range(len(given)),
    )
    index, orient, fine, spots = outs[:4]
    outs = outs[4:]
    state, first, second, star, left, proj, tab, pick, far, chip, own = outs[:11]
    got_chip, got_far, got_off = trade(far, chip, outs[11:], n_fault, n_off)
    part, coef, fnbr, left_all, lift, here, pick_here, pick_far, flags, source = call(
        functools.partial(side_kernel, n_off),
        (
            first,
            star,
            tab,
            jnp.transpose(flux_local, (1, 2, 0, 3)),
            jnp.transpose(flux_nbr, (1, 2, 0, 3)),
            stiff_vol,
            flux_minus,
            face_turn,
            jnp.transpose(face_lift, (1, 0, 2)),
            index,
            orient,
            fine,
            spots,
            jnp.transpose(source_term, (1, 0, 2)),
        ),
        [
            wide,
            shape(7 * 16, W),
            shape(Q * 16, LANES),
            shape(2 * M, 7 * M + 8, dtype=BF16),
            shape(2 * M, 12 * JP, dtype=BF16),
            near,
            shape(LANES, LANES, dtype=BF16),
            shape(2 * rows, LANES, dtype=BF16),
            shape(8, LANES, dtype=jnp.int32),
            wide,
        ],
        [
            vmem((7 * M + 8, W), F32),
            vmem((512, LANES), F32),
            vmem((3 * JP, LANES), F32),
            vmem((LANES, LANES), F32),
            vmem((8, LANES), jnp.int32),
        ],
    )
    outs = call(
        functools.partial(middle_kernel, n_off),
        (state, second, part, here, fnbr, flags, lift, star, left, proj, pick, pick_far, own, got_chip, got_far, *got_off),
        [near, wide, wide, table] + [block] * (3 + n_off - 1),
        [vmem((M, W), F32), vmem((12 * JP, W), F32), vmem((rows, TAB), F32), vmem((M, W), F32)],
    )
    near_first, half, later, tab, far, chip, own = outs[:7]
    got_chip, got_far, got_off = trade(far, chip, outs[7:], n_fault, n_off)
    base, here = call(
        late_side_kernel,
        (first, second, later, half, source, near_first, tab, coef, left_all, flags, pick_here),
        [wide, near],
        [vmem((M, W), F32), vmem((7 * M + 8, W), F32)],
    )
    (result,) = call(
        functools.partial(last_kernel, n_off),
        (base, here, fnbr, flags, lift, pick_far, own, got_chip, got_far, *got_off),
        [shape(Q, E, M)],
        [vmem((Q * JP + 8, LANES), F32), vmem((12 * JP, W), F32), vmem((rows, TAB), F32), vmem((LANES, W), F32)],
    )
    return jnp.transpose(result, (0, 2, 1))


def solution(mesh):
    n_fault, n_off = mesh.shape["fault"], mesh.shape["off"]
    both = ("fault", "off")
    in_specs = (
        P(None, None, both),
        P(None, None, None, both),
        P(None, None, None, both),
        P(None, None, None, both),
        P(),
        P(),
        P(),
        P(),
        P(),
        P(),
        P(both),
        P("fault", "off", None),
        P("fault", "off", None),
        P(None, both),
        P(None, both),
        P(),
        P(),
    )
    return jax.shard_map(
        functools.partial(on_device, n_fault, n_off),
        mesh=mesh,
        in_specs=in_specs,
        out_specs=P(None, None, both),
        check_vma=False,
    )
```

```python
import functools
import math

import jax
import jax.numpy as jnp
from jax import lax
from jax.experimental import pallas as pl
from jax.experimental.pallas import tpu as pltpu
from jax.sharding import PartitionSpec as P


Q = 9
M = 56
J = 21
JP = 24
E = 32
LANES = 128
W = 384
SO = 10
SRC = 16
TERMS = 6
EARLY = [0.5 ** (k + 1) / math.factorial(k + 1) for k in range(TERMS)]
LATE = [(1.0 - 0.5 ** (k + 1)) / math.factorial(k + 1) for k in range(TERMS)]
F32 = jnp.float32
BF16 = jnp.bfloat16
TAB = 256


def lane_iota(rows, width=LANES):
    return lax.broadcasted_iota(jnp.int32, (rows, width), 1)


def row_iota(rows, width=LANES):
    return lax.broadcasted_iota(jnp.int32, (rows, width), 0)


def halves(rows):
    lane = lane_iota(rows)
    return lane < 64, (lane & 32) == 0


def roll(x, shift):
    return pltpu.roll(x, shift, 1)


def split(x):
    high = x.astype(BF16)
    low = (x - high.astype(F32)).astype(BF16)
    return high, low


def dot(a, b):
    return lax.dot_general(a, b, (((1,), (0,)), ((), ())), preferred_element_type=F32)


def dot_nt(a, b):
    return lax.dot_general(a, b, (((1,), (1,)), ((), ())), preferred_element_type=F32)


def product(left, right):
    high, low = split(right)
    rows = left.shape[0] // 2
    width = right.shape[1]
    wide = dot(left, jnp.concatenate([high, low], axis=1))
    return wide[:rows, :width] + (wide[rows:, :width] + wide[:rows, width:])


def stack_split(x):
    high, low = split(x)
    return jnp.concatenate([high.astype(F32), low.astype(F32)], axis=0).astype(BF16)


def turns(columns):
    first, even = halves(8)
    tiles = []
    for column in columns[:2]:
        tiles += [column] + [roll(column, 128 - 32 * s) for s in range(1, 4)]
    pair = jnp.where(first, columns[2], roll(columns[2], 64))
    return tiles + [jnp.where(even, pair, roll(pair, 32))]


def group_swap(parts):
    first, even = halves(8)
    a0, a1, a2, a3 = parts
    out = []
    p = [jnp.where(first, a0, roll(a2, 64)), jnp.where(first, a1, roll(a3, 64))]
    r = [jnp.where(first, roll(a0, 64), a2), jnp.where(first, roll(a1, 64), a3)]
    for x, y in (p, r):
        out.append(jnp.where(even, x, roll(y, 32)))
        out.append(jnp.where(even, roll(x, 96), y))
    return out


def place_rows(source, target, start, members):
    def piece(q, d, group):
        order = [4 * c + (group + s) % 4 for c in range(2) for s in range(4)] + [Q - 1]
        return jnp.concatenate([source[q, p : p + 1, d, :] for p in order], axis=0)

    for d in members:
        for c in range(2):
            target[start + d * 16 : start + d * 16 + Q, c * 128 : c * 128 + 128] = group_place(
                [piece(4 * c + g, d, g) for g in range(4)]
            )
    target[start : start + Q, 256:W] = group_place([piece(Q - 1, d, g) for g, d in enumerate(members)])


def group_place(parts):
    if len(parts) < 4:
        parts = parts + [jnp.zeros((parts[0].shape[0], E * (4 - len(parts))), parts[0].dtype)]
    return jnp.concatenate(parts, axis=1)


def weigh(rows_of, x_ref, y_ref, count):
    for tile in range(M // 8):
        spans = turns([x_ref[tile * 8 : tile * 8 + 8, c * 128 : c * 128 + 128] for c in range(3)])

        def mixed(row, column):
            total = rows_of[row : row + 1, column : column + 128] * spans[0]
            for p in (4, 1, 5, 2, 6, 3, 7, 8):
                total = total + rows_of[row + p : row + p + 1, column : column + 128] * spans[p]
            return total

        for d in range(count):
            start = (tile * count + d) * 8
            for c in range(2):
                y_ref[start : start + 8, c * 128 : c * 128 + 128] = mixed(d * 16, c * 128)
        for pack in range(0, count, 4):
            total = mixed(pack * 16, 256)
            for d in range(pack, min(pack + 4, count)):
                start = (tile * count + d) * 8
                moved = roll(total, 128 - 32 * (d - pack)) if d > pack else total
                y_ref[start : start + 8, 256:W] = moved


def order_rows(tall, matrices):
    for d, matrix in enumerate(matrices):
        for tile in range(M // 8):
            start = (tile * len(matrices) + d) * 8
            tall[start : start + 8, 0:M] = matrix[tile * 8 : tile * 8 + 8]


def predict(star, left, x_ref, y_ref, first_ref, second_ref):
    y_ref[3 * M : 3 * M + 8, :] = jnp.zeros((8, W), F32)
    state = x_ref[...]
    first_ref[...] = EARLY[0] * state
    if second_ref is not None:
        second_ref[...] = LATE[0] * state
    for k in range(1, TERMS):
        weigh(star, x_ref, y_ref, 3)
        result = product(left[...], y_ref[0 : 3 * M + 8, :])
        x_ref[...] = result
        first_ref[...] = first_ref[...] + EARLY[k] * result
        if second_ref is not None:
            second_ref[...] = second_ref[...] + LATE[k] * result


def make_table(project, x, tab_ref):
    high = x.astype(BF16).astype(F32)
    faced = dot(project, jnp.concatenate([high, high, x - high], axis=0).astype(BF16))
    for tile in range(3):
        for c in range(3):
            parts = [
                faced[f * JP + tile * 8 : f * JP + tile * 8 + 8, c * 128 : c * 128 + 128] for f in range(4)
            ]
            swapped = group_swap(parts)
            for g in range(4 if c < 2 else 1):
                row = (c * 4 + g) * JP + tile * 8
                tab_ref[row : row + 8, :] = swapped[g]
    tab_ref[Q * JP : TAB, :] = jnp.zeros((TAB - Q * JP, LANES), F32)


def send_rows(pick, tab_ref):
    high, low = split(tab_ref[...])
    return dot_nt(jnp.concatenate([pick, pick], axis=1), jnp.concatenate([high, low], axis=1))


def off_rank():
    return lax.axis_index("off")


def turned_around():
    return 16 - 16 * lax.rem(lax.axis_index("fault"), 2)


def put_sends(rows, far_ref, chip_ref, self_ref, off_refs):
    chip_ref[...] = rows[0:16]
    far_ref[...] = rows[16:32]
    self_ref[...] = rows[32:48]
    for k, ref in enumerate(off_refs):
        ref[...] = rows[48 + 16 * k : 64 + 16 * k]


def first_kernel(n_off, *refs):
    sources = refs[:10]
    landed = refs[-7:-1] + refs[10:14]
    copies = [
        pltpu.make_async_copy(source, target, refs[-1].at[k])
        for k, (source, target) in enumerate(zip(sources, landed))
    ]
    for copy in copies:
        copy.start()
    state_in, star_in, stiff_in, proj_in, elem_in, face_in = landed[:6]
    refs = refs[14:-7]
    (state_out, first_out, second_out, star_out, left_out, proj_out, tab_out, pick_out, far, chip, own) = refs[:11]
    offs = refs[11 : 11 + n_off - 1]
    x_ref, y_ref, tall, slot_pad = refs[11 + n_off - 1 :]
    tall[...] = jnp.zeros((W, LANES), F32)
    slot_pad[...] = jnp.zeros((8, LANES), jnp.int32)
    for copy in copies:
        copy.wait()
    for q in range(Q):
        tall[q * E : q * E + E, 0:M] = state_in[q]
    x_ref[:, Q * E : W] = jnp.zeros((M, W - Q * E), F32)
    x_ref[:, 0 : Q * E] = tall[0 : Q * E, :].T[0:M]
    state_out[...] = x_ref[...]
    star_out[...] = jnp.zeros((48, W), F32)
    place_rows(star_in, star_out, 0, range(3))
    tall[...] = jnp.zeros((W, LANES), F32)
    order_rows(tall, [stiff_in[d] for d in range(3)])
    left_out[...] = stack_split(tall[0 : 3 * M + 8, :].T[0:M])
    tall[0 : 4 * JP, :] = jnp.zeros((4 * JP, LANES), F32)
    for f in range(4):
        tall[f * JP : f * JP + J, 0:M] = proj_in[:, f, :]
    values = tall[0 : 4 * JP, 0:M]
    high = values.astype(BF16).astype(F32)
    proj_out[...] = jnp.concatenate([high, values - high, high], axis=1).astype(BF16)
    slots = elem_in.shape[2]
    slot_pad[0:1, 0:slots] = face_in[0] * E + elem_in[0] + 1
    rows = 32 + 16 * n_off
    row = row_iota(rows)
    block = row >> 4
    within = row & 15
    target = lax.rem(block - 2 + off_rank(), n_off)
    slot = jnp.where(row < 32, row ^ turned_around(), jnp.where(within < SO, 32 + target * SO + within, -1))
    wanted = jnp.where(lane_iota(rows) == slot, slot_pad[0:1, :], 0)
    entry = jnp.sum(wanted.astype(F32), axis=1, keepdims=True)
    pick = jnp.where(lane_iota(rows).astype(F32) + 1.0 == entry, 1.0, 0.0).astype(BF16)
    pick_out[...] = pick

    predict(star_out, left_out, x_ref, y_ref, first_out, second_out)
    make_table(proj_out[...], first_out[...], tab_out)
    put_sends(send_rows(pick, tab_out), far, chip, own, offs)


def gather_local(pick, tab_ref):
    high, low = split(tab_ref[0 : Q * JP + 8, :])
    return dot(jnp.concatenate([high, low], axis=1), jnp.concatenate([pick, pick], axis=0))


def side_kernel(
    n_off,
    first_in,
    star,
    tab,
    local_in,
    nbr_in,
    vol_in,
    minus_in,
    turn_in,
    lift_in,
    index_in,
    orient_in,
    cluster_in,
    source_elem,
    source_in,
    part_out,
    coef_out,
    fnbr_out,
    left_out,
    lift_out,
    here_out,
    pick_here_out,
    pick_far_out,
    flags_out,
    source_out,
    y_ref,
    tall,
    turn_pad,
    lift_pad,
    ipad,
):
    coef_out[...] = jnp.zeros((7 * 16, W), F32)
    place_rows(local_in, coef_out, 0, range(4))
    coef_out[4 * 16 : 7 * 16, :] = star[...]
    for q in range(Q):
        fnbr_out[q * 16 : q * 16 + Q, :] = group_place([nbr_in[q, :, f, :] for f in range(4)])
    tall[...] = jnp.zeros((512, LANES), F32)
    order_rows(tall, [minus_in[f] for f in range(4)] + [vol_in[d] for d in range(3)])
    left_out[...] = stack_split(tall[...].T[0:M, 0 : 7 * M + 8])
    turn_pad[...] = jnp.zeros((3 * JP, LANES), F32)
    for o in range(3):
        turn_pad[o * JP : o * JP + J, 0:J] = turn_in[o]
    tall[...] = jnp.zeros((512, LANES), F32)
    lift_pad[...] = jnp.zeros((LANES, LANES), F32)
    for f in range(4):
        lift_pad[0:J, 0:M] = lift_in[:, f, :]
        combined = lax.dot_general(
            turn_pad[...],
            lift_pad[...],
            (((1,), (0,)), ((), ())),
            precision=lax.Precision.HIGHEST,
            preferred_element_type=F32,
        )
        for o in range(3):
            for tile in range(3):
                start = (tile * 12 + f * 3 + o) * 8
                tall[start : start + 8, :] = combined[o * JP + tile * 8 : o * JP + tile * 8 + 8]
    lift_out[...] = stack_split(tall[...].T[0:M, 0 : 12 * JP])
    ipad[...] = jnp.zeros((8, LANES), jnp.int32)
    index_row = group_place([index_in[f : f + 1, :] for f in range(4)])
    ipad[0:4, 0:E] = orient_in[...]
    ipad[4:5, 0:E] = cluster_in[...]
    orient = ipad[...]
    twice = orient + roll(orient, 64)
    flags_out[...] = twice + roll(twice, 32)
    pick_here = jnp.where(row_iota(LANES) == index_row, 1.0, 0.0).astype(BF16)
    pick_here_out[...] = pick_here
    rows = 32 + 16 * n_off
    row = row_iota(rows)
    within = row & 15
    source = lax.rem(off_rank() + n_off + 2 - (row >> 4), n_off)
    place = jnp.where(
        row < 32, LANES + (row ^ turned_around()), jnp.where(within < SO, LANES + 32 + source * SO + within, -1)
    )
    pick_far = jnp.where(place == index_row, 1.0, 0.0)
    pick_far_out[...] = jnp.concatenate([pick_far, pick_far], axis=0).astype(BF16)
    here_out[...] = gather_local(pick_here, tab)
    tall[...] = jnp.zeros((512, LANES), F32)
    for q in range(Q):
        tall[q * SRC : q * SRC + SRC, 0:M] = source_in[q]
    origin = (lax.axis_index("fault") * n_off + off_rank()) * E
    row = row_iota(SRC)
    ipad[0:1, 0:SRC] = source_elem[...] - origin
    lane = lane_iota(SRC)
    here = jnp.where(lane == row, ipad[0:1, :], 0).astype(F32)
    goal = jnp.sum(here, axis=1, keepdims=True).astype(jnp.int32)
    y_ref[0 : Q * SRC, :] = jnp.zeros((Q * SRC, W), F32)
    for q in range(Q):
        lane_in = lane - 32 * (q % 4)
        hit = jnp.logical_and(lane_in == goal, jnp.logical_and(goal >= 0, goal < E))
        c = q // 4
        y_ref[q * SRC : q * SRC + SRC, c * 128 : c * 128 + 128] = jnp.where(hit, 1.0, 0.0)
    picks = y_ref[0 : Q * SRC, :].astype(BF16)
    terms = tall[0:256, :].T[0:M, 0 : Q * SRC]
    high, low = split(terms)
    rest = (terms - high.astype(F32) - low.astype(F32)).astype(BF16)
    source_out[...] = dot(high, picks) + (dot(low, picks) + dot(rest, picks))

    weigh(coef_out, first_in, y_ref, 7)
    y_ref[7 * M : 7 * M + 8, :] = jnp.zeros((8, W), F32)
    part_out[...] = product(left_out[...], y_ref[...])


def arrive(n_off, chip, far, own, offs, pick_far, stage):
    stage[0:16, :] = chip[0][...] + chip[1][...]
    stage[16:32, :] = far[...]
    stage[32:48, :] = own[...]
    for k in range(n_off - 1):
        stage[48 + 16 * k : 64 + 16 * k, :] = offs[2 * k][...] + offs[2 * k + 1][...]
    rows = stage[...]
    high = rows.astype(BF16).astype(F32)
    turned = jnp.concatenate([high, rows - high], axis=0).T[0 : Q * JP + 8, :].astype(BF16)
    return dot(turned, pick_far[...])


def neighbour_flux(near_ref, fnbr, flags, lift, y_ref):
    for tile in range(3):
        near = [near_ref[p * JP + tile * 8 : p * JP + tile * 8 + 8, :] for p in range(Q)]
        fluxes = []
        for q in range(Q):
            total = fnbr[q * 16 : q * 16 + 1, :] * near[0]
            for p in range(1, Q):
                total = total + fnbr[q * 16 + p : q * 16 + p + 1, :] * near[p]
            fluxes.append(total)
        zero = jnp.zeros((8, LANES), F32)
        for c in range(3):
            parts = [fluxes[4 * c + g] if 4 * c + g < Q else zero for g in range(4)]
            swapped = group_swap(parts)
            for f in range(4):
                facing = flags[f : f + 1, :]
                for o in range(3):
                    start = (tile * 12 + f * 3 + o) * 8
                    y_ref[start : start + 8, c * 128 : c * 128 + 128] = jnp.where(
                        facing == o, swapped[f], 0.0
                    )
    return product(lift[...], y_ref[0 : 12 * JP, :])


def wide_fine(flags):
    row = flags[4:5, :] == 1
    return row


def middle_kernel(
    n_off, state, second, part, here, fnbr, flags, lift, star, left, proj, pick, pick_far, own, lead, rest, far, *refs
):
    chip = (lead, rest)
    offs = refs[: 2 * (n_off - 1)]
    outs = refs[2 * (n_off - 1) :]
    near_out, half_out, later_out, tab_out, far_out, chip_out, own_out = outs[:7]
    off_outs = outs[7 : 7 + n_off - 1]
    x_ref, y_ref, stage, acc = outs[7 + n_off - 1 :]
    near_out[...] = here[...] + arrive(n_off, chip, far, own, offs, pick_far, stage)
    total = part[...] + neighbour_flux(near_out, fnbr, flags, lift, y_ref)
    fine = jnp.concatenate([wide_fine(flags)] * 3, axis=1)
    base = state[...]
    half = jnp.where(fine, base + total, base)
    half_out[...] = half
    x_ref[...] = half
    predict(star, left, x_ref, y_ref, acc, None)
    later = jnp.where(fine, acc[...], second[...])
    later_out[...] = later
    make_table(proj[...], later, tab_out)
    put_sends(send_rows(pick[...], tab_out), far_out, chip_out, own_out, off_outs)


def late_side_kernel(
    first, second, later, half, source, near_first, tab, coef, left, flags, pick_here, base_out, here_out, x_ref, y_ref
):
    row = wide_fine(flags)
    fine = jnp.concatenate([row] * 3, axis=1)
    x_ref[...] = jnp.where(fine, later[...], first[...] + second[...])
    weigh(coef, x_ref, y_ref, 7)
    y_ref[7 * M : 7 * M + 8, :] = jnp.zeros((8, W), F32)
    base_out[...] = half[...] + source[...] + product(left[...], y_ref[...])
    here_out[...] = gather_local(pick_here[...], tab) + jnp.where(row, 0.0, near_first[...])


def last_kernel(n_off, base, here, fnbr, flags, lift, pick_far, own, lead, rest, far, *refs):
    chip = (lead, rest)
    offs = refs[: 2 * (n_off - 1)]
    out, near, y_ref, stage, tall = refs[2 * (n_off - 1) :]
    tall[M:LANES, :] = jnp.zeros((LANES - M, W), F32)
    near[...] = here[...] + arrive(n_off, chip, far, own, offs, pick_far, stage)
    total = base[...] + neighbour_flux(near, fnbr, flags, lift, y_ref)
    tall[0:M, :] = total
    turned = tall[...].T
    for q in range(Q):
        out[q] = turned[q * E : q * E + E, 0:M]


def shape(*dims, dtype=F32):
    return jax.ShapeDtypeStruct(dims, dtype)


def call(kernel, ins, outs, scratch, smem=(), hbm=(), cost=2000000):
    specs = [
        pl.BlockSpec(
            memory_space=pltpu.SMEM if k in smem else pltpu.HBM if k in hbm else pltpu.VMEM
        )
        for k in range(len(ins))
    ]
    return pl.pallas_call(
        kernel,
        in_specs=specs,
        out_specs=[pl.BlockSpec(memory_space=pltpu.VMEM)] * len(outs),
        out_shape=outs,
        scratch_shapes=scratch,
        compiler_params=pltpu.CompilerParams(vmem_limit_bytes=16 * 1024 * 1024),
        cost_estimate=pl.CostEstimate(flops=cost * 1000, bytes_accessed=cost, transcendentals=0),
    )(*ins)


def trade(far, chip, offs, n_fault, n_off):
    both = ("fault", "off")

    def chip_pairs(firsts):
        pairs = [(i, (i + 1) % n_fault) for i in firsts]
        return [(a * n_off + j, b * n_off + j) for i, k in pairs for a, b in ((i, k), (k, i)) for j in range(n_off)]

    def off_pairs(ranks, step):
        return [(i * n_off + j, i * n_off + (j + step) % n_off) for i in ranks for j in range(n_off)]

    chips, offs_got = [], [[] for _ in offs]
    chips.append(lax.ppermute(chip, both, chip_pairs([0])))
    for k, rows in enumerate(offs):
        offs_got[k].append(lax.ppermute(rows, both, off_pairs([0], k + 1)))
    got_far = lax.ppermute(far, both, chip_pairs(range(1, n_fault, 2)))
    chips.append(lax.ppermute(chip, both, chip_pairs(range(2, n_fault, 2))))
    for k, rows in enumerate(offs):
        offs_got[k].append(lax.ppermute(rows, both, off_pairs(range(1, n_fault), k + 1)))
    return chips, got_far, sum(offs_got, [])


def on_device(
    n_fault,
    n_off,
    modal_state,
    star_mats,
    flux_local,
    flux_nbr,
    stiff_time,
    stiff_vol,
    flux_minus,
    face_proj,
    face_turn,
    face_lift,
    cluster,
    send_elem,
    send_face,
    nbr_index,
    orientation,
    source_elem,
    source_term,
):
    vmem = pltpu.VMEM
    rows = 32 + 16 * n_off
    wide = shape(M, W)
    table = shape(TAB, LANES)
    block = shape(16, TAB)
    near = shape(Q * JP + 8, LANES)
    given = (
        jnp.transpose(modal_state, (0, 2, 1)),
        jnp.transpose(star_mats, (1, 2, 0, 3)),
        stiff_time,
        jnp.transpose(face_proj, (2, 0, 1)),
        send_elem,
        send_face,
        nbr_index,
        orientation,
        cluster.reshape(1, E),
        source_elem.reshape(1, SRC),
    )
    outs = call(
        functools.partial(first_kernel, n_off),
        [pltpu.with_memory_space_constraint(x, pltpu.HBM) for x in given],
        [shape(*x.shape, dtype=x.dtype) for x in given[6:]]
        + [
            wide,
            wide,
            wide,
            shape(48, W),
            shape(2 * M, 3 * M + 8, dtype=BF16),
            shape(4 * JP, 3 * M, dtype=BF16),
            table,
            shape(rows, LANES, dtype=BF16),
        ]
        + [block] * (3 + n_off - 1),
        [
            vmem((M, W), F32),
            vmem((3 * M + 8, W), F32),
            vmem((W, LANES), F32),
            vmem((8, LANES), jnp.int32),
        ]
        + [vmem(x.shape, x.dtype) for x in given[:6]]
        + [pltpu.SemaphoreType.DMA((len(given),))],
        hbm=range(len(given)),
    )
    index, orient, fine, spots = outs[:4]
    outs = outs[4:]
    state, first, second, star, left, proj, tab, pick, far, chip, own = outs[:11]
    got_chip, got_far, got_off = trade(far, chip, outs[11:], n_fault, n_off)
    part, coef, fnbr, left_all, lift, here, pick_here, pick_far, flags, source = call(
        functools.partial(side_kernel, n_off),
        (
            first,
            star,
            tab,
            jnp.transpose(flux_local, (1, 2, 0, 3)),
            jnp.transpose(flux_nbr, (1, 2, 0, 3)),
            stiff_vol,
            flux_minus,
            face_turn,
            jnp.transpose(face_lift, (1, 0, 2)),
            index,
            orient,
            fine,
            spots,
            jnp.transpose(source_term, (1, 0, 2)),
        ),
        [
            wide,
            shape(7 * 16, W),
            shape(Q * 16, LANES),
            shape(2 * M, 7 * M + 8, dtype=BF16),
            shape(2 * M, 12 * JP, dtype=BF16),
            near,
            shape(LANES, LANES, dtype=BF16),
            shape(2 * rows, LANES, dtype=BF16),
            shape(8, LANES, dtype=jnp.int32),
            wide,
        ],
        [
            vmem((7 * M + 8, W), F32),
            vmem((512, LANES), F32),
            vmem((3 * JP, LANES), F32),
            vmem((LANES, LANES), F32),
            vmem((8, LANES), jnp.int32),
        ],
    )
    outs = call(
        functools.partial(middle_kernel, n_off),
        (state, second, part, here, fnbr, flags, lift, star, left, proj, pick, pick_far, own, *got_chip, got_far, *got_off),
        [near, wide, wide, table] + [block] * (3 + n_off - 1),
        [vmem((M, W), F32), vmem((12 * JP, W), F32), vmem((rows, TAB), F32), vmem((M, W), F32)],
    )
    near_first, half, later, tab, far, chip, own = outs[:7]
    got_chip, got_far, got_off = trade(far, chip, outs[7:], n_fault, n_off)
    base, here = call(
        late_side_kernel,
        (first, second, later, half, source, near_first, tab, coef, left_all, flags, pick_here),
        [wide, near],
        [vmem((M, W), F32), vmem((7 * M + 8, W), F32)],
    )
    (result,) = call(
        functools.partial(last_kernel, n_off),
        (base, here, fnbr, flags, lift, pick_far, own, *got_chip, got_far, *got_off),
        [shape(Q, E, M)],
        [vmem((Q * JP + 8, LANES), F32), vmem((12 * JP, W), F32), vmem((rows, TAB), F32), vmem((LANES, W), F32)],
    )
    return jnp.transpose(result, (0, 2, 1))


def solution(mesh):
    n_fault, n_off = mesh.shape["fault"], mesh.shape["off"]
    both = ("fault", "off")
    in_specs = (
        P(None, None, both),
        P(None, None, None, both),
        P(None, None, None, both),
        P(None, None, None, both),
        P(),
        P(),
        P(),
        P(),
        P(),
        P(),
        P(both),
        P("fault", "off", None),
        P("fault", "off", None),
        P(None, both),
        P(None, both),
        P(),
        P(),
    )
    return jax.shard_map(
        functools.partial(on_device, n_fault, n_off),
        mesh=mesh,
        in_specs=in_specs,
        out_specs=P(None, None, both),
        check_vma=False,
    )
```
